32 devices in a mesh: dp: 4 (over y, x), expert: 8 (over z, core).
Axes of the slice: x: 2, y: 2, z: 4, core: 2. Of those that a mesh axis runs over, the one named last changes fastest.
Arguments:
- tables: float32 [4, 8192, 256], P(None, ('dp', 'expert')), may hold values from -3 to 3
- accum: float32 [4, 8192], P(None, ('dp', 'expert')), may hold values from 0.01 to 1
- bag_owner: int32 [4096, 16], P(('dp', 'expert')), may hold values from 0 to 31, all different within a row; in each aligned block of 128 rows (0 to 127, 128 to 255, ...) at most 81 rows name the same one
- bag_row: int32 [4096, 16], P(('dp', 'expert')), may hold values from 0 to 255
- bag_len: int32 [4, 4096], P(None, ('dp', 'expert')), may hold values from 1 to 4, 10240 in all within a row
- route: int32 [4096, 2], P(('dp', 'expert')), may hold values from 0 to 7, all different within a row; in each aligned block of 128 rows (0 to 127, 128 to 255, ...) at most 33 rows name the same one
- labels: float32 [4096, 2], P(('dp', 'expert')), may hold values from 0 to 1
- w_in: bfloat16 [8, 1024, 2048], P('expert', None, 'dp'), may hold values from -0.1875 to 0.1875
- w_out: bfloat16 [8, 2048, 1024], P('expert', 'dp'), may hold values from -0.125 to 0.125
- gate_w: bfloat16 [2, 1024, 8], replicated, may hold values from -0.1875 to 0.1875
- head: float32 [2, 1024], replicated, may hold values from -0.375 to 0.375
Outputs:
- logits: float32 [4096, 2], P(('dp', 'expert'))
- new_tables: float32 [4, 8192, 256], P(None, ('dp', 'expert'))
- new_accum: float32 [4, 8192], P(None, ('dp', 'expert'))
The draws below stay inside these ranges and needn't reach their ends.
Inputs may be any that keep to these rules, and one draw needn't show every extreme that they name: `bag_owner`: each sample names 16 different owners; the rows of one device name any one owner at most 81 times. `route`: each sample names two different experts; the rows of one device name any one expert at most 33 times.
All inputs are finite; a program needn't handle non-finite values. No bound on the sum of `bag_len` on one device may be relied on, other than what follows from the above.
Results may differ from the reference program's by a relative error of at most 0.0062.
Values may be sent and summed in bfloat16 or wider, within the bound.
No kernel may reach another device: no remote copies, remote signals or barrier semaphores. Data moves between devices by JAX's collectives and lax.ppermute only.
A program may use at most 128 MiB of HBM per device.

```python
import math
import jax
import jax.numpy as jnp
import numpy as np
from jax import lax

EDIM = 256
TABLES = 4
ROWS_DEV = 256
BAG = 4
HID = 2048
TASKS = 2
S_DEV = 128
TROWS = 8192
SAMPLES = 4096
D = 1024
EXPERTS = 8
CAP_E = 33
CAP_R = 81
N_DP = 4
N_EXPERT = 8


def touch_ends(result, stream_key, smallest, high):
    longest = result.shape.index(max(result.shape))
    spots = []
    for shift in (0, 1):
        where = [jax.random.randint(jax.random.fold_in(stream_key, axis), (), 0, length) for axis, length in enumerate(result.shape)]
        where[longest] = (where[longest] + shift) % result.shape[longest]
        spots.append(tuple(where))
    return result.at[spots[0]].set(smallest).at[spots[1]].set(high)


def levels(stream_key, extent, shards, smallest, top_value):
    level, own = 1.0, jax.random.fold_in(stream_key, 6)
    for dim, parts in shards:
        steps = jnp.exp(jax.random.uniform(jax.random.fold_in(own, dim), (parts,), jnp.float32, smallest / len(shards), top_value / len(shards)))
        level = level * jnp.repeat(steps, extent[dim] // parts).reshape([-1 if axis == dim else 1 for axis in range(len(extent))])
    return level


def rank_bounds(number_of, slope):
    loads = [(1 << 20) // math.isqrt(grade ** slope) + 1 for grade in range(1, number_of + 1)]
    scale = 1 + sum(loads) // (1 << 30)
    return np.cumsum(np.array([max(1, weight // scale) for weight in loads]))


def skewed_ids(stream_key, shape, number_of, slope):
    grid = rank_bounds(number_of, slope)
    ticket = jax.random.randint(jax.random.fold_in(stream_key, 1), shape, 0, int(grid[number_of - 1]))
    grade = jnp.searchsorted(jnp.asarray(grid, jnp.int32), ticket, side="right")
    return jax.random.permutation(jax.random.fold_in(stream_key, 2), number_of)[grade].astype(jnp.int32)


def profile(number_of, total, bound, skew):
    loads = [(1 << 20) // math.isqrt(standing ** skew) + 1 for standing in range(2, number_of + 1)]
    rest, holding = total - bound - (number_of - 1), [1] * (number_of - 1)
    while rest > 0:
        free = [i for i in range(number_of - 1) if holding[i] < bound]
        whole, budget = sum([loads[i] for i in free]), rest
        for i in free:
            addition = min(bound - holding[i], max(1, budget * loads[i] // whole), rest)
            holding[i] = holding[i] + addition
            rest = rest - addition
    return np.array([bound] + holding)


def uneven_parts(key, count, total, bound, skew):
    if count == 2:
        one = jax.random.randint(key, (), max(1, total - bound), min(bound, total - 1) + 1)
        return jnp.stack([one, total - one])
    sizes = jnp.asarray(profile(count, total, bound, skew), jnp.int32)
    twos = (count - 1) // 2
    giver, sink = sizes[1:1 + 2 * twos:2], sizes[2:2 + 2 * twos:2]
    slack = jnp.minimum(giver - 1, bound - sink)
    moved = jax.random.randint(jax.random.fold_in(key, 1), (twos,), 0, 1 << 20) % (slack + 1)
    sizes = sizes.at[1:1 + 2 * twos:2].set(giver - moved).at[2:2 + 2 * twos:2].set(sink + moved)
    return sizes[jax.random.permutation(jax.random.fold_in(key, 2), count)]


def routed_block(own_key, own, number, rows, count, top, limit, slope):
    order = jax.random.permutation(own_key, count)
    crowded, common = shares(count, rows * top, limit, slope, True), shares(count, rows * top, limit, slope, False)
    places = jnp.arange(count)

    def named(tallies, rotation):
        used = int((tallies > 0).sum())
        fixed = max(1, used // 4)
        shifted = fixed + (places - fixed + rotation * (used - fixed)) % max(1, count - fixed)
        return jnp.zeros((count,), jnp.int32).at[order[jnp.where(places < fixed, places, shifted)]].set(jnp.asarray(tallies, jnp.int32))

    tallies = jnp.where(number % 4 == 0, named(crowded, number // 4), named(common, number - number // 4 - 1))
    mixed = jax.random.permutation(jax.random.fold_in(own, 3), count)
    source_of, taker = mixed[0:count // 2 * 2:2], mixed[1:count // 2 * 2:2]
    margin = jnp.minimum(tallies[source_of] - 1, limit - tallies[taker]) // 2
    margin = jnp.where((source_of == order[0]) | (taker == order[0]) | (tallies[taker] == 0), 0, jnp.maximum(margin, 0))
    shifted = jax.random.randint(jax.random.fold_in(own, 4), (count // 2,), 0, 1 << 20) % (margin + 1)
    tallies = tallies.at[source_of].add(-shifted).at[taker].add(shifted)
    items = jnp.searchsorted(jnp.cumsum(tallies), jnp.arange(rows * top), side="right").astype(jnp.int32)
    grid = items.reshape(top, rows).T
    grid = grid[jax.random.permutation(jax.random.fold_in(own, 1), rows)]
    rotation = jax.random.randint(jax.random.fold_in(own, 2), (rows, 1), 0, top)
    return jnp.take_along_axis(grid, (jnp.arange(top)[None, :] + rotation) % top, axis=1)


def shares(count, total, most, skew, full):
    portions = [(1 << 20) // math.isqrt(rank ** skew) + 1 for rank in range(1, count + 1)]
    largest = most if full else min(most, max(-(-total // count), total * portions[0] // sum(portions)))
    least = 1 if total - largest >= count - 1 else 0
    counts, spare = [largest] + [least] * (count - 1), total - largest - least * (count - 1)
    while spare > 0:
        movable = [i for i in range(1, count) if counts[i] < largest] or [i for i in range(1, count) if counts[i] < most]
        mass, budget = sum([portions[i] for i in movable]), spare
        for i in movable:
            more = min(most - counts[i], max(1, budget * portions[i] // mass), spare)
            counts[i] = counts[i] + more
            spare = spare - more
    return np.array(counts)


def bell_draw(key, shape, spread, bound, cuts=(), held_as=jnp.bfloat16):
    result = spread * jax.random.normal(key, shape, jnp.float32)
    if cuts:
        result = result * levels(key, shape, cuts, -0.22, 0.18)
    return jnp.clip(result, -bound, bound).astype(held_as)


def setup_inputs(seed: int = 0) -> dict:
    keys = jax.random.split(jax.random.key(seed), 12)
    tables = bell_draw(keys[0], (TABLES, TROWS, EDIM), 0.5, 3.0, ((1, 32),), jnp.float32)
    accum = jnp.clip(jnp.exp(math.log(1.0) - 4.6051702 * jax.random.uniform(keys[1], (TABLES, TROWS), jnp.float32) ** levels(keys[1], (TABLES, TROWS), ((1, 32),), -0.2, 0.2)), 0.01, 1.0)
    bag_owner_keys = jax.random.split(jax.random.fold_in(keys[2], 1), SAMPLES // S_DEV)
    bag_owner_turns = jax.random.permutation(jax.random.fold_in(keys[2], 3), SAMPLES // S_DEV)
    bag_owner = jax.vmap(lambda own, number: routed_block(jax.random.fold_in(keys[2], 2), own, number, S_DEV, N_DP * N_EXPERT, TABLES * BAG, CAP_R, 2))(bag_owner_keys, bag_owner_turns).reshape((SAMPLES, TABLES * BAG))
    bag_row = touch_ends(skewed_ids(keys[3], (SAMPLES, TABLES * BAG), ROWS_DEV, 2), jax.random.fold_in(keys[3], 3), 0, ROWS_DEV - 1).astype(jnp.int32)
    bag_len = jax.vmap(lambda own: uneven_parts(own, SAMPLES, SAMPLES * 5 // 2, BAG, 1))(jax.random.split(keys[4], TABLES)).reshape((TABLES, SAMPLES)).astype(jnp.int32)
    route_keys = jax.random.split(jax.random.fold_in(keys[5], 1), SAMPLES // S_DEV)
    route_turns = jax.random.permutation(jax.random.fold_in(keys[5], 3), SAMPLES // S_DEV)
    route = jax.vmap(lambda own, number: routed_block(jax.random.fold_in(keys[5], 2), own, number, S_DEV, EXPERTS, 2, CAP_E, 2))(route_keys, route_turns).reshape((SAMPLES, 2))
    labels = jnp.clip(1.0 * jax.random.uniform(keys[6], (SAMPLES, TASKS), jnp.float32) ** levels(keys[6], (SAMPLES, TASKS), ((0, 32),), -0.2, 0.2), 0.0, 1.0)
    w_in = bell_draw(keys[7], (EXPERTS, D, HID), D ** -0.5, 0.1875, ((0, 8), (2, 4)))
    w_out = bell_draw(keys[8], (EXPERTS, HID, D), HID ** -0.5, 0.125, ((0, 8), (1, 4)))
    gate_w = bell_draw(keys[9], (TASKS, D, EXPERTS), D ** -0.5, 0.1875)
    head = bell_draw(keys[10], (TASKS, D), (D // 4) ** -0.5, 0.375, (), jnp.float32)
    return dict(tables=tables, accum=accum, bag_owner=bag_owner, bag_row=bag_row, bag_len=bag_len, route=route, labels=labels, w_in=w_in, w_out=w_out, gate_w=gate_w, head=head)


learn_rate = 0.3
norm_eps = 1e-05

def slot_rank(dest, buckets):
    count = dest.shape[0]
    order = jnp.argsort(dest, stable=True).astype(jnp.int32)
    ordered = dest[order]
    starts = jnp.searchsorted(ordered, jnp.arange(buckets, dtype=jnp.int32), side='left').astype(jnp.int32)
    within = jnp.arange(count, dtype=jnp.int32) - starts[ordered]
    return jnp.zeros((count,), jnp.int32).at[order].set(within)

def reference(tables, accum, bag_owner, bag_row, bag_len, route, labels, w_in, w_out, gate_w, head):
    device_count = SAMPLES // S_DEV
    gid = (bag_owner * ROWS_DEV + bag_row).reshape(SAMPLES, TABLES, BAG)
    live = jnp.arange(BAG, dtype=jnp.int32)[None, None, :] < bag_len.T[:, :, None]
    table_ix = jnp.arange(TABLES, dtype=jnp.int32)[None, :, None]

    def pool_block(pair):
        ids, alive = pair
        rows = tables[table_ix, ids]
        return lax.optimization_barrier(jnp.sum(jnp.where(alive[..., None], rows, 0.0), axis=2))
    pooled = lax.map(pool_block, (gid.reshape(device_count, S_DEV, TABLES, BAG), live.reshape(device_count, S_DEV, TABLES, BAG)))
    features = pooled.reshape(SAMPLES, D).astype(jnp.bfloat16)
    experts_flat = route.reshape(-1)
    rank = slot_rank(experts_flat, EXPERTS)
    slots = device_count * CAP_E
    sample_of = jnp.arange(2 * SAMPLES, dtype=jnp.int32) // 2
    buffer = jnp.zeros((EXPERTS, slots, D), jnp.bfloat16).at[experts_flat, rank].set(features[sample_of])

    def forward_one(trip):
        rows, first_w, second_w = trip
        pre = jnp.dot(rows, first_w, preferred_element_type=jnp.float32)
        hidden = jnp.maximum(pre, 0.0).astype(jnp.bfloat16)
        return jnp.dot(hidden, second_w, preferred_element_type=jnp.float32).astype(jnp.bfloat16)
    outputs = lax.map(forward_one, (buffer, w_in, w_out))
    picked = outputs[experts_flat, rank].reshape(SAMPLES, 2, D).astype(jnp.float32)
    scores = jnp.einsum('sd,tde->ste', features.astype(jnp.float32), gate_w.astype(jnp.float32), precision=lax.Precision.HIGHEST)
    chosen = jnp.take_along_axis(scores, jnp.broadcast_to(route[:, None, :], (SAMPLES, TASKS, 2)), axis=2)
    first = jax.nn.sigmoid(chosen[..., 0] - chosen[..., 1])
    gates = jnp.stack([first, 1.0 - first], axis=-1)
    combined = jnp.einsum('stk,skd->std', gates, picked, precision=lax.Precision.HIGHEST)
    scale = jnp.sqrt(lax.optimization_barrier(jnp.mean(combined * combined, axis=-1, keepdims=True)) + norm_eps)
    normed = combined / scale
    logits = lax.optimization_barrier(jnp.sum(normed * head[None], axis=-1))
    dlogit = jax.nn.sigmoid(logits) - labels
    dnormed = dlogit[..., None] * head[None]
    dcomb = (dnormed - normed * lax.optimization_barrier(jnp.mean(dnormed * normed, axis=-1, keepdims=True))) / scale
    dpicked = jnp.einsum('stk,std->skd', gates, dcomb, precision=lax.Precision.HIGHEST).astype(jnp.bfloat16)
    dgates = jnp.einsum('std,skd->stk', dcomb, picked, precision=lax.Precision.HIGHEST)
    ddelta = (dgates[..., 0] - dgates[..., 1]) * first * (1.0 - first)
    onehot = (route[:, :, None] == jnp.arange(EXPERTS, dtype=jnp.int32)[None, None, :]).astype(jnp.float32)
    dscores = ddelta[:, :, None] * (onehot[:, None, 0, :] - onehot[:, None, 1, :])
    dgate_in = jnp.einsum('ste,tde->sd', dscores, gate_w.astype(jnp.float32), precision=lax.Precision.HIGHEST)
    dbuffer = jnp.zeros((EXPERTS, slots, D), jnp.bfloat16).at[experts_flat, rank].set(dpicked.reshape(-1, D))

    def backward_one(quad):
        rows, grads, first_w, second_w = quad
        pre = jnp.dot(rows, first_w, preferred_element_type=jnp.float32)
        dhidden = jnp.dot(grads, second_w.T, preferred_element_type=jnp.float32)
        dpre = jnp.where(pre > 0.0, dhidden, 0.0).astype(jnp.bfloat16)
        return jnp.dot(dpre, first_w.T, preferred_element_type=jnp.float32).astype(jnp.bfloat16)
    dinputs = lax.map(backward_one, (buffer, dbuffer, w_in, w_out))
    dexpert = dinputs[experts_flat, rank].reshape(SAMPLES, 2, D).astype(jnp.float32)
    dfeatures = dgate_in + lax.optimization_barrier(jnp.sum(dexpert, axis=1))
    dpooled = dfeatures.reshape(SAMPLES, TABLES, EDIM)
    updates = jnp.where(live[..., None], dpooled[:, :, None, :], 0.0)
    row_grads = jnp.zeros((TABLES, TROWS, EDIM), jnp.float32).at[table_ix, gid].add(updates)
    new_accum = accum + lax.optimization_barrier(jnp.mean(row_grads * row_grads, axis=-1))
    new_tables = tables - learn_rate * row_grads / jnp.sqrt(new_accum)[..., None]
    return (logits, new_tables, new_accum)
```

```python
import jax
import jax.numpy as jnp
from jax import lax
from jax.experimental import pallas as pl
from jax.experimental.pallas import tpu as pltpu
from jax.sharding import PartitionSpec as P

learn_rate = 0.3
norm_eps = 1e-05
LANES = 128
F32 = jnp.float32
BF16 = jnp.bfloat16
I32 = jnp.int32


def vmem(count):
    return [pl.BlockSpec(memory_space=pltpu.VMEM)] * count


def params():
    return pltpu.CompilerParams(vmem_limit_bytes=60 << 20)


def seq(count, body):
    if count <= 32:
        for i in range(count):
            body(i)
    else:
        lax.fori_loop(0, count, lambda i, c: (body(i), c)[1], 0)


class Slots:
    def __init__(self, peers, cap, width, group):
        self.peers, self.width = peers, width
        self.main, self.ext = (cap - 1, 1) if cap % 16 == 1 else (-(-cap // 16) * 16, 0)
        self.lane_blocks = width // LANES
        self.group = min(peers, group)
        self.blocks = peers // self.group
        self.rows = self.group * (self.main + self.ext)
        self.ext_units = -(-self.lane_blocks // 8) * 8 * self.ext
        self.units = self.main * self.lane_blocks + self.ext_units

    def pick(self, axis):
        shape = (self.group, self.rows) if axis == 1 else (self.rows, self.group)
        c = lax.broadcasted_iota(I32, shape, axis)
        o = lax.broadcasted_iota(I32, shape, 1 - axis)
        base = o * self.main
        bulk = self.group * self.main
        own = (c >= base) & (c < base + self.main)
        rank = c - base + 1
        if self.ext:
            own = own | (c == bulk + o)
            rank = jnp.where(c < bulk, rank, self.main + 1)
        expand = jnp.where(own, 1.0, 0.0).astype(BF16)
        rank = jnp.sum(jnp.where(own, rank.astype(F32), 0.0), axis=1 - axis, keepdims=True)
        return expand, rank

    def spread(self, ranks, picks):
        expand, rank = picks
        held = jnp.dot(ranks.astype(BF16), expand, preferred_element_type=F32)
        return jnp.where(held == rank, 1.0, 0.0).astype(BF16)

    def spread_t(self, ranks, picks):
        expand, rank = picks
        held = lax.dot_general(
            expand, ranks.astype(BF16), (((1,), (1,)), ((), ())), preferred_element_type=F32
        )
        return jnp.where(held == rank, 1.0, 0.0).astype(BF16)

    def ext_pick(self, j):
        shape = (self.group * self.ext_units, self.group)
        u = lax.broadcasted_iota(I32, shape, 0)
        o = lax.broadcasted_iota(I32, shape, 1)
        return jnp.where(u == o * self.ext_units + j, 1.0, 0.0).astype(BF16)

    def pack(self, block, rows_ref, out_ref):
        main, first = self.main, block * self.group

        def one(o):
            start = o * main if isinstance(o, int) else pl.multiple_of(o * main, 16)
            for j in range(self.lane_blocks):
                out_ref[first + o, j * main : (j + 1) * main, :] = rows_ref[
                    pl.ds(start, main), j * LANES : (j + 1) * LANES
                ]

        seq(self.group, one)
        if self.ext:
            extra = jnp.zeros((self.group * self.ext_units, LANES), F32)
            tail = rows_ref[self.group * main : self.rows, :]
            for j in range(self.lane_blocks):
                extra = extra + jnp.dot(
                    self.ext_pick(j), tail[:, j * LANES : (j + 1) * LANES], preferred_element_type=F32
                )
            extra = extra.reshape(self.group, self.ext_units, LANES).astype(BF16)
            out_ref[first : first + self.group, self.lane_blocks * main : self.units, :] = extra

    def unpack(self, block, in_ref, rows_ref):
        main, first = self.main, block * self.group

        def one(o):
            start = o * main if isinstance(o, int) else pl.multiple_of(o * main, 16)
            for j in range(self.lane_blocks):
                rows_ref[pl.ds(start, main), j * LANES : (j + 1) * LANES] = in_ref[
                    first + o, j * main : (j + 1) * main, :
                ]

        seq(self.group, one)
        if self.ext:
            extra = in_ref[first : first + self.group, self.lane_blocks * main : self.units, :]
            extra = extra.astype(F32).reshape(self.group * self.ext_units, LANES).astype(BF16)
            for j in range(self.lane_blocks):
                rows_ref[self.group * main : self.rows, j * LANES : (j + 1) * LANES] = (
                    lax.dot_general(
                        self.ext_pick(j),
                        extra,
                        (((0,), (0,)), ((), ())),
                        preferred_element_type=F32,
                    ).astype(BF16)
                )


def one_hot_rows(slots, block, want_ref, hot_ref):
    group, main = slots.group, slots.main
    want = want_ref[block * group : (block + 1) * group, :].astype(F32)
    fill = jnp.zeros((LANES - group, LANES), F32)
    cols = jnp.concatenate([want, fill], axis=0).T
    entry = lax.broadcasted_iota(I32, (main, hot_ref.shape[1]), 1).astype(F32)
    for o in range(group):
        hit = cols[0:main, o : o + 1] == entry
        hot_ref[o * main : (o + 1) * main, :] = jnp.where(hit, 1.0, 0.0).astype(BF16)
    if slots.ext:
        entry = lax.broadcasted_iota(I32, (group, hot_ref.shape[1]), 1).astype(F32)
        hit = want[:, main : main + 1] == entry
        hot_ref[group * main : slots.rows, :] = jnp.where(hit, 1.0, 0.0).astype(BF16)


def index_kernel(cap, table_rows, owner_ref, row_ref, len_ref, route_ref, rank_ref, want_ref, erank_ref, tmp_ref):
    tables, samples, owners = rank_ref.shape
    experts = erank_ref.shape[2]
    slots = owner_ref.shape[1] // tables
    owner, row, length, route = owner_ref[...], row_ref[...], len_ref[...], route_ref[...]
    peer = lax.broadcasted_iota(I32, (samples, owners), 1)
    entry = jnp.zeros((samples, owners), F32)
    named = []
    for t in range(tables):
        mine = jnp.zeros((samples, owners), F32)
        for b in range(slots):
            j = t * slots + b
            hit = (owner[:, j : j + 1] == peer) & (length[:, t : t + 1] > b)
            mine = mine + jnp.where(hit, 1.0, 0.0)
            entry = entry + jnp.where(hit, (row[:, j : j + 1] + (t * table_rows + 1)).astype(F32), 0.0)
        named.append(mine)
    every = sum(named)
    before = (
        lax.broadcasted_iota(I32, (samples, samples), 0) > lax.broadcasted_iota(I32, (samples, samples), 1)
    )
    before = jnp.where(before, 1.0, 0.0).astype(BF16)
    rank = jnp.dot(before, every.astype(BF16), preferred_element_type=F32) + 1.0
    for t in range(tables):
        rank_ref[t] = named[t] * rank
    rank = every * rank
    tmp_ref[...] = jnp.zeros(tmp_ref.shape, F32)
    for r in range(cap):
        tmp_ref[r : r + 1, 0:owners] = jnp.sum(
            jnp.where(rank == float(r + 1), entry, 0.0), axis=0, keepdims=True
        )
    want_ref[...] = tmp_ref[...].T[0:owners, :].astype(I32) - 1
    expert = lax.broadcasted_iota(I32, (samples, experts), 1)
    hits = [jnp.where(route[:, k : k + 1] == expert, 1.0, 0.0) for k in range(2)]
    rank = jnp.dot(before, (hits[0] + hits[1]).astype(BF16), preferred_element_type=F32) + 1.0
    for k in range(2):
        erank_ref[k] = hits[k] * rank


def gather_kernel(slots, want_ref, table_ref, out_ref, hot_ref, rows_ref):
    table = table_ref[...].astype(BF16)
    for block in range(slots.blocks):
        one_hot_rows(slots, block, want_ref, hot_ref)
        rows_ref[...] = jnp.dot(hot_ref[...], table, preferred_element_type=F32).astype(BF16)
        slots.pack(block, rows_ref, out_ref)


def pool_kernel(slots, eslots, got_ref, rank_ref, erank_ref, gate_ref, out_ref, first_ref, rows_ref, feat_ref, send_ref):
    tables = rank_ref.shape[0]
    width = slots.width
    group = slots.group
    picks = slots.pick(1)
    sums = [0.0] * tables
    for block in range(slots.blocks):
        slots.unpack(block, got_ref, rows_ref)
        rows = rows_ref[...]
        for t in range(tables):
            ranks = rank_ref[t, :, block * group : (block + 1) * group]
            sums[t] = sums[t] + jnp.dot(slots.spread(ranks, picks), rows, preferred_element_type=F32)
    for t in range(tables):
        feat_ref[:, t * width : (t + 1) * width] = sums[t].astype(BF16)
    feats = feat_ref[...]
    eranks = [erank_ref[k] for k in range(2)]
    hot = eslots.spread_t(eranks[0] + eranks[1], eslots.pick(0))
    send_ref[...] = jnp.dot(hot, feats, preferred_element_type=F32).astype(BF16)
    eslots.pack(0, send_ref, out_ref)
    for t in range(first_ref.shape[1]):
        score = lax.dot_general(feats, gate_ref[t], (((1,), (1,)), ((), ())), preferred_element_type=F32)
        z = [jnp.sum(jnp.where(eranks[k] > 0.0, score, 0.0), axis=1, keepdims=True) for k in range(2)]
        first_ref[:, t : t + 1] = jax.nn.sigmoid(z[0] - z[1])


def weight_parts(refs, buf):
    half = buf.shape[1] // 2
    return [
        (refs[0], buf.at[0]),
        (refs[1], buf.at[1]),
        (refs[2], buf.at[2]),
        (refs[3], buf.at[3, 0:half]),
        (refs[4], buf.at[3, half : 2 * half]),
    ]


def start_weights(in_refs, out_refs, in_buf, out_buf, sems):
    ins, outs = weight_parts(in_refs, in_buf), weight_parts(out_refs, out_buf)
    waits = [[] for _ in range(4)]
    for i in range(5):
        for n, (source, target) in enumerate((ins[i], outs[i])):
            copy = pltpu.make_async_copy(source, target, sems.at[2 * i + n])
            copy.start()
            waits[min(i, 3)].append(copy)
    return waits


def forward_kernel(eslots, x_ref, *refs):
    in_refs, out_refs = refs[0:5], refs[5:10]
    y_ref, hidden_ref, rows_ref, in_buf, out_buf, sems = refs[10:]
    waits = start_weights(in_refs, out_refs, in_buf, out_buf, sems)
    eslots.unpack(0, x_ref, rows_ref)
    rows = rows_ref[...]
    total = 0.0
    for i in range(4):
        for copy in waits[i]:
            copy.wait()
        pre = jnp.dot(rows, in_buf[i], preferred_element_type=F32)
        hidden = jnp.maximum(pre, 0.0).astype(BF16)
        hidden_ref[i] = hidden
        total = total + jnp.dot(hidden, out_buf[i], preferred_element_type=F32)
    rows_ref[...] = total.astype(BF16)
    eslots.pack(0, rows_ref, y_ref)


def backward_kernel(eslots, dy_ref, hidden_ref, *refs):
    in_refs, out_refs = refs[0:5], refs[5:10]
    dx_ref, rows_ref, in_buf, out_buf, sems = refs[10:]
    waits = start_weights(in_refs, out_refs, in_buf, out_buf, sems)
    eslots.unpack(0, dy_ref, rows_ref)
    rows = rows_ref[...]
    total = 0.0
    nt = (((1,), (1,)), ((), ()))
    for i in range(4):
        for copy in waits[i]:
            copy.wait()
        dhidden = lax.dot_general(rows, out_buf[i], nt, preferred_element_type=F32)
        dpre = jnp.where(hidden_ref[i].astype(F32) > 0.0, dhidden, 0.0).astype(BF16)
        total = total + lax.dot_general(dpre, in_buf[i], nt, preferred_element_type=F32)
    rows_ref[...] = total.astype(BF16)
    eslots.pack(0, rows_ref, dx_ref)


def middle_kernel(eslots, y_ref, erank_ref, first_ref, label_ref, head_ref, gate_ref, logit_ref, dgate_ref, out_ref, rows_ref):
    tasks = first_ref.shape[1]
    width = eslots.width
    eslots.unpack(0, y_ref, rows_ref)
    rows = rows_ref[...]
    eranks = [erank_ref[k] for k in range(2)]
    picks = eslots.pick(1)
    y0, y1 = [
        jnp.dot(eslots.spread(eranks[k], picks), rows, preferred_element_type=F32) for k in range(2)
    ]
    gap = y0 - y1
    hits = [jnp.where(eranks[k] > 0.0, 1.0, 0.0) for k in range(2)]
    sign = hits[0] - hits[1]
    dy0 = dy1 = dgate = 0.0
    for t in range(tasks):
        g = first_ref[:, t : t + 1]
        rest = 1.0 - g
        comb = g * y0 + rest * y1
        scale = jnp.sqrt(jnp.sum(comb * comb, axis=1, keepdims=True) * (1.0 / width) + norm_eps)
        inv = 1.0 / scale
        normed = comb * inv
        head = head_ref[t : t + 1, :]
        logit = jnp.sum(normed * head, axis=1, keepdims=True)
        logit_ref[:, t : t + 1] = logit
        dlogit = jax.nn.sigmoid(logit) - label_ref[:, t : t + 1]
        drop = dlogit * logit * (1.0 / width)
        dcomb = (dlogit * head - normed * drop) * inv
        dy0 = dy0 + g * dcomb
        dy1 = dy1 + rest * dcomb
        ddelta = jnp.sum(dcomb * gap, axis=1, keepdims=True) * g * rest
        dgate = dgate + jnp.dot(
            ddelta * sign,
            gate_ref[t].astype(F32),
            precision=lax.Precision.HIGHEST,
            preferred_element_type=F32,
        )
    dgate_ref[...] = dgate
    picks = eslots.pick(0)
    send = sum(
        jnp.dot(eslots.spread_t(eranks[k], picks), dy.astype(BF16), preferred_element_type=F32)
        for k, dy in enumerate((dy0, dy1))
    )
    rows_ref[...] = send.astype(BF16)
    eslots.pack(0, rows_ref, out_ref)


def spread_grads_kernel(slots, eslots, dx_ref, erank_ref, dgate_ref, rank_ref, out_ref, rows_ref, grad_ref):
    tables = rank_ref.shape[0]
    width, group = slots.width, slots.group
    eslots.unpack(0, dx_ref, rows_ref)
    total = dgate_ref[...] + spread_pair(eslots, erank_ref, rows_ref)
    total = total.astype(BF16)
    picks = slots.pick(0)
    for block in range(slots.blocks):
        grads = 0.0
        for t in range(tables):
            ranks = rank_ref[t, :, block * group : (block + 1) * group]
            grads = grads + jnp.dot(
                slots.spread_t(ranks, picks), total[:, t * width : (t + 1) * width], preferred_element_type=F32
            )
        grad_ref[...] = grads.astype(BF16)
        slots.pack(block, grad_ref, out_ref)


def spread_pair(eslots, erank_ref, rows_ref):
    picks = eslots.pick(1)
    rows = rows_ref[...]
    hot = eslots.spread(erank_ref[0], picks) + eslots.spread(erank_ref[1], picks)
    return jnp.dot(hot, rows, preferred_element_type=F32)


def update_kernel(slots, got_ref, want_ref, table_ref, accum_ref, new_table_ref, new_accum_ref, hot_ref, rows_ref):
    tables, table_rows = accum_ref.shape
    width = slots.width
    grads = 0.0
    for block in range(slots.blocks):
        one_hot_rows(slots, block, want_ref, hot_ref)
        slots.unpack(block, got_ref, rows_ref)
        grads = grads + lax.dot_general(
            rows_ref[...], hot_ref[...], (((0,), (0,)), ((), ())), preferred_element_type=F32
        )
    for t in range(tables):
        part = grads[:, t * table_rows : (t + 1) * table_rows]
        total = accum_ref[t : t + 1, :] + jnp.sum(part * part, axis=0, keepdims=True) * (1.0 / width)
        new_accum_ref[t : t + 1, :] = total
        step = part * (learn_rate / jnp.sqrt(total))
        new_table_ref[t] = table_ref[t] - step.T


def gather_weight(w):
    flip = lambda bit: [(i, i ^ bit) for i in range(4)]
    half = w.shape[0] // 2
    by1 = lax.ppermute(w, "dp", flip(1))
    by2 = lax.ppermute(w, "dp", flip(2))
    low = lax.ppermute(by1[:half], "dp", flip(2))
    high = lax.ppermute(by2[half:], "dp", flip(1))
    return [w, by1, by2, low, high]


def per_device(
    tables, accum, bag_owner, bag_row, bag_len, route, labels, w_in, w_out, gate_w, head
):
    dp_count = lax.axis_size("dp")
    expert_count = lax.axis_size("expert")
    device_count = dp_count * expert_count
    samples = route.shape[0]
    table_count, table_rows, emb = tables.shape
    entries = table_count * table_rows
    lookups = samples * bag_owner.shape[1]
    width = table_count * emb
    tasks = labels.shape[1]
    cap_rows = (5 * lookups + 4 * device_count - 1) // (4 * device_count) + 1
    cap_expert = (2 * samples + expert_count - 1) // expert_count + 1
    slots = Slots(device_count, cap_rows, emb, 32)
    eslots = Slots(expert_count, cap_expert, width, expert_count)
    shape = jax.ShapeDtypeStruct
    both = ("dp", "expert")

    ins = gather_weight(w_in[0])
    outs = gather_weight(w_out[0])

    def call(kernel, out_shape, scratch, *args, **kw):
        many = isinstance(out_shape, (list, tuple))
        return pl.pallas_call(
            kernel,
            out_shape=out_shape,
            in_specs=kw.get("in_specs", vmem(len(args))),
            out_specs=vmem(len(out_shape)) if many else vmem(1)[0],
            scratch_shapes=scratch,
            compiler_params=params(),
            name=kw["name"],
        )(*args)

    def bind(fn, *static):
        return lambda *refs: fn(*static, *refs)

    rank, want, erank = call(
        bind(index_kernel, cap_rows, table_rows),
        [
            shape((table_count, samples, device_count), F32),
            shape((device_count, LANES), I32),
            shape((2, samples, expert_count), F32),
        ],
        [pltpu.VMEM((LANES, max(LANES, device_count)), F32)],
        bag_owner,
        bag_row,
        bag_len.T,
        route,
        name="index",
    )
    gate_t = jnp.swapaxes(gate_w, 1, 2)
    wanted = lax.all_to_all(want, both, 0, 0, tiled=True)
    row_shape = shape((device_count, slots.units, LANES), BF16)
    exp_shape = shape((expert_count, eslots.units, LANES), BF16)
    hot = pltpu.VMEM((slots.rows, entries), BF16)
    rows = pltpu.VMEM((slots.rows, emb), BF16)
    erows = pltpu.VMEM((eslots.rows, width), BF16)
    served = call(
        bind(gather_kernel, slots), row_shape, [hot, rows], wanted, tables.reshape(entries, emb), name="gather"
    )
    returned = lax.all_to_all(served, both, 0, 0, tiled=True)
    outgoing, first = call(
        bind(pool_kernel, slots, eslots),
        [exp_shape, shape((samples, tasks), F32)],
        [rows, pltpu.VMEM((samples, width), BF16), erows],
        returned,
        rank,
        erank,
        gate_t,
        name="pool",
    )
    arrived = lax.all_to_all(outgoing, "expert", 0, 0, tiled=True)
    share = w_in.shape[2]
    anywhere = [pl.BlockSpec(memory_space=pl.ANY)] * 10
    weights = [
        pltpu.VMEM((4, width, share), BF16),
        pltpu.VMEM((4, share, width), BF16),
        pltpu.SemaphoreType.DMA((10,)),
    ]
    result, hidden = call(
        bind(forward_kernel, eslots),
        [exp_shape, shape((4, eslots.rows, share), BF16)],
        [erows] + weights,
        arrived,
        *ins,
        *outs,
        in_specs=vmem(1) + anywhere,
        name="forward",
    )
    back = lax.all_to_all(result, "expert", 0, 0, tiled=True)
    logits, dgate, grads_out = call(
        bind(middle_kernel, eslots),
        [shape((samples, tasks), F32), shape((samples, width), F32), exp_shape],
        [erows],
        back,
        erank,
        first,
        labels,
        head,
        gate_t,
        name="middle",
    )
    arrived_grads = lax.all_to_all(grads_out, "expert", 0, 0, tiled=True)
    dinput = call(
        bind(backward_kernel, eslots),
        exp_shape,
        [erows] + weights,
        arrived_grads,
        hidden,
        *ins,
        *outs,
        in_specs=vmem(2) + anywhere,
        name="backward",
    )
    back_grads = lax.all_to_all(dinput, "expert", 0, 0, tiled=True)
    row_out = call(
        bind(spread_grads_kernel, slots, eslots),
        row_shape,
        [erows, rows],
        back_grads,
        erank,
        dgate,
        rank,
        name="spread",
    )
    row_in = lax.all_to_all(row_out, both, 0, 0, tiled=True)
    new_tables, new_accum = call(
        bind(update_kernel, slots),
        [shape(tables.shape, F32), shape(accum.shape, F32)],
        [hot, rows],
        row_in,
        wanted,
        tables,
        accum,
        name="update",
    )
    return (logits, new_tables, new_accum)


def solution(mesh):
    in_specs = (
        P(None, ("dp", "expert"), None),
        P(None, ("dp", "expert")),
        P(("dp", "expert"), None),
        P(("dp", "expert"), None),
        P(None, ("dp", "expert")),
        P(("dp", "expert"), None),
        P(("dp", "expert"), None),
        P("expert", None, "dp"),
        P("expert", "dp", None),
        P(),
        P(),
    )
    out_specs = (
        P(("dp", "expert"), None),
        P(None, ("dp", "expert"), None),
        P(None, ("dp", "expert")),
    )
    return jax.shard_map(
        per_device, mesh=mesh, in_specs=in_specs, out_specs=out_specs, check_vma=False
    )
```

```python
import jax
import jax.numpy as jnp
from jax import lax
from jax.experimental import pallas as pl
from jax.experimental.pallas import tpu as pltpu
from jax.sharding import PartitionSpec as P


learn_rate = 0.3
norm_eps = 1e-05
LANES = 128
F32 = jnp.float32
BF16 = jnp.bfloat16
I32 = jnp.int32


def vmem(count):
    return [pl.BlockSpec(memory_space=pltpu.VMEM)] * count


def hbm(count):
    return [pl.BlockSpec(memory_space=pltpu.HBM)] * count


def params(mib):
    return pltpu.CompilerParams(vmem_limit_bytes=mib << 20)


def seq(count, body):
    if count <= 32:
        for i in range(count):
            body(i)
    else:
        lax.fori_loop(0, count, lambda i, c: (body(i), c)[1], 0)


def part(refs, o, a, b):
    return refs[o].at[a:b, :] if isinstance(refs, (list, tuple)) else refs.at[o, a:b, :]


class Slots:
    def __init__(self, peers, cap, width, group, apart=False):
        self.apart = apart
        self.peers, self.width = peers, width
        self.main, self.ext = (cap - 1, 1) if cap % 16 == 1 else (-(-cap // 16) * 16, 0)
        self.lane_blocks = width // LANES
        self.group = min(peers, group)
        self.blocks = peers // self.group
        self.rows = self.group * (self.main + self.ext)
        self.ext_units = -(-self.lane_blocks // 8) * 8 * self.ext
        self.units = self.main * self.lane_blocks + self.ext_units

    @property
    def arrays(self):
        return self.peers if self.apart else 1

    def refs(self, refs):
        return refs[0 : self.peers] if self.apart else refs[0]

    def shapes(self):
        if self.apart:
            return [jax.ShapeDtypeStruct((self.units, LANES), BF16)] * self.peers
        return [jax.ShapeDtypeStruct((self.peers, self.units, LANES), BF16)]

    def pick(self, axis):
        shape = (self.group, self.rows) if axis == 1 else (self.rows, self.group)
        c = lax.broadcasted_iota(I32, shape, axis)
        o = lax.broadcasted_iota(I32, shape, 1 - axis)
        base = o * self.main
        bulk = self.group * self.main
        own = (c >= base) & (c < base + self.main)
        rank = c - base + 1
        if self.ext:
            own = own | (c == bulk + o)
            rank = jnp.where(c < bulk, rank, self.main + 1)
        expand = jnp.where(own, 1.0, 0.0).astype(BF16)
        rank = jnp.sum(jnp.where(own, rank.astype(F32), 0.0), axis=1 - axis, keepdims=True)
        return expand, rank

    def spread(self, ranks, picks):
        expand, rank = picks
        held = jnp.dot(ranks.astype(BF16), expand, preferred_element_type=F32)
        return jnp.where(held == rank, 1.0, 0.0).astype(BF16)

    def spread_t(self, ranks, picks):
        expand, rank = picks
        held = lax.dot_general(
            expand, ranks.astype(BF16), (((1,), (1,)), ((), ())), preferred_element_type=F32
        )
        return jnp.where(held == rank, 1.0, 0.0).astype(BF16)

    def ext_pick(self, j):
        shape = (self.group * self.ext_units, self.group)
        u = lax.broadcasted_iota(I32, shape, 0)
        o = lax.broadcasted_iota(I32, shape, 1)
        return jnp.where(u == o * self.ext_units + j, 1.0, 0.0).astype(BF16)

    def pack(self, block, rows_ref, out_ref):
        main, first = self.main, block * self.group

        def one(o):
            start = o * main if isinstance(o, int) else pl.multiple_of(o * main, 16)
            for j in range(self.lane_blocks):
                part(out_ref, first + o, j * main, (j + 1) * main)[...] = rows_ref[
                    pl.ds(start, main), j * LANES : (j + 1) * LANES
                ]

        seq(self.group, one)
        if self.ext:
            extra = jnp.zeros((self.group * self.ext_units, LANES), F32)
            tail = rows_ref[self.group * main : self.rows, :]
            for j in range(self.lane_blocks):
                extra = extra + jnp.dot(
                    self.ext_pick(j), tail[:, j * LANES : (j + 1) * LANES], preferred_element_type=F32
                )
            for o in range(self.group):
                part(out_ref, first + o, self.lane_blocks * main, self.units)[...] = extra[
                    o * self.ext_units : (o + 1) * self.ext_units
                ].astype(BF16)

    def unpack(self, block, in_ref, rows_ref):
        main, first = self.main, block * self.group

        def one(o):
            start = o * main if isinstance(o, int) else pl.multiple_of(o * main, 16)
            for j in range(self.lane_blocks):
                rows_ref[pl.ds(start, main), j * LANES : (j + 1) * LANES] = part(
                    in_ref, first + o, j * main, (j + 1) * main
                )[...]

        seq(self.group, one)
        if self.ext:
            extra = [
                part(in_ref, first + o, self.lane_blocks * main, self.units)[...].astype(F32)
                for o in range(self.group)
            ]
            extra = jnp.concatenate(extra, axis=0).astype(BF16)
            for j in range(self.lane_blocks):
                rows_ref[self.group * main : self.rows, j * LANES : (j + 1) * LANES] = (
                    lax.dot_general(
                        self.ext_pick(j),
                        extra,
                        (((0,), (0,)), ((), ())),
                        preferred_element_type=F32,
                    ).astype(BF16)
                )


def one_hot_rows(slots, block, want_ref, hot_ref):
    group, main = slots.group, slots.main
    want = want_ref[block * group : (block + 1) * group, :].astype(F32)
    fill = jnp.zeros((LANES - group, LANES), F32)
    cols = jnp.concatenate([want, fill], axis=0).T
    entry = lax.broadcasted_iota(I32, (main, hot_ref.shape[1]), 1).astype(F32)
    for o in range(group):
        hit = cols[0:main, o : o + 1] == entry
        hot_ref[o * main : (o + 1) * main, :] = jnp.where(hit, 1.0, 0.0).astype(BF16)
    if slots.ext:
        entry = lax.broadcasted_iota(I32, (group, hot_ref.shape[1]), 1).astype(F32)
        hit = want[:, main : main + 1] == entry
        hot_ref[group * main : slots.rows, :] = jnp.where(hit, 1.0, 0.0).astype(BF16)


def index_kernel(cap, table_rows, me_ref, owner_ref, row_ref, len_ref, route_ref, rank_ref, want_ref, erank_ref, stage_ref, tmp_ref, sems):
    tables, samples, owners = rank_ref.shape
    experts = erank_ref.shape[2]
    columns = owner_ref.shape[0]
    slots = columns // tables
    lines = (0, columns, 2 * columns, 2 * columns + 8)
    counts = (columns, columns, tables, 2)
    copies = [
        pltpu.make_async_copy(ref, stage_ref.at[line : line + count, :], sems.at[i])
        for i, (ref, line, count) in enumerate(zip((owner_ref, row_ref, len_ref, route_ref), lines, counts))
    ]
    for copy in copies:
        copy.start()
    tmp_ref[...] = jnp.zeros(tmp_ref.shape, F32)
    for copy in copies:
        copy.wait()
    for line, count in zip(lines, counts):
        tmp_ref[line : line + count, 0:samples] = stage_ref[line : line + count, :].astype(F32)
    args = tmp_ref[:, 0:samples].T
    peer = lax.broadcasted_iota(I32, (samples, owners), 1).astype(F32)
    entry = jnp.zeros((samples, owners), F32)
    named = []
    for t in range(tables):
        mine = jnp.zeros((samples, owners), F32)
        length = args[:, 2 * columns + t : 2 * columns + t + 1]
        for b in range(slots):
            j = t * slots + b
            live = jnp.where(length > float(b), args[:, j : j + 1], -1.0)
            hit = live == peer
            mine = jnp.where(hit, 1.0, mine)
            entry = jnp.where(hit, args[:, columns + j : columns + j + 1] + float(t * table_rows + 1), entry)
        named.append(mine)
    every = sum(named)
    before = (
        lax.broadcasted_iota(I32, (samples, samples), 0) > lax.broadcasted_iota(I32, (samples, samples), 1)
    )
    before = jnp.where(before, 1.0, 0.0).astype(BF16)
    rank = jnp.dot(before, every.astype(BF16), preferred_element_type=F32) + 1.0
    for t in range(tables):
        rank_ref[t] = named[t] * rank
    rank = every * rank
    tmp_ref[...] = jnp.zeros(tmp_ref.shape, F32)
    for r in range(cap):
        tmp_ref[r : r + 1, 0:owners] = jnp.sum(
            jnp.where(rank == float(r + 1), entry, 0.0), axis=0, keepdims=True
        )
    want_ref[...] = tmp_ref[...].T[0:owners, :].astype(I32) - 1
    expert = lax.broadcasted_iota(I32, (samples, experts), 1)
    routes = [args[:, 2 * columns + 8 + k : 2 * columns + 9 + k] for k in range(2)]
    for k in range(2):
        erank_ref[2 + k] = jnp.where(routes[k] == expert.astype(F32), 1.0, 0.0)
    expert = (expert ^ me_ref[0]).astype(F32)
    hits = [jnp.where(routes[k] == expert, 1.0, 0.0) for k in range(2)]
    rank = jnp.dot(before, (hits[0] + hits[1]).astype(BF16), preferred_element_type=F32) + 1.0
    for k in range(2):
        erank_ref[k] = hits[k] * rank


def gather_kernel(slots, want_ref, table_ref, out_ref, held_ref, hot_ref, rows_ref, sem):
    copy = pltpu.make_async_copy(table_ref, held_ref, sem)
    copy.start()
    for block in range(slots.blocks):
        one_hot_rows(slots, block, want_ref, hot_ref)
        if block == 0:
            copy.wait()
        rows_ref[...] = jnp.dot(
            hot_ref[...], held_ref[...].astype(BF16), preferred_element_type=F32
        ).astype(BF16)
        slots.pack(block, rows_ref, out_ref)


def pool_kernel(slots, eslots, got_ref, rank_ref, erank_ref, gate_ref, *refs):
    out_ref = eslots.refs(refs)
    first_ref, rows_ref, feat_ref, send_ref = refs[eslots.arrays :]
    tables = rank_ref.shape[0]
    width = slots.width
    group = slots.group
    picks = slots.pick(1)
    sums = [0.0] * tables
    for block in range(slots.blocks):
        slots.unpack(block, got_ref, rows_ref)
        rows = rows_ref[...]
        for t in range(tables):
            ranks = rank_ref[t, :, block * group : (block + 1) * group]
            sums[t] = sums[t] + jnp.dot(slots.spread(ranks, picks), rows, preferred_element_type=F32)
    for t in range(tables):
        feat_ref[:, t * width : (t + 1) * width] = sums[t].astype(BF16)
    feats = feat_ref[...]
    eranks = [erank_ref[k] for k in range(2)]
    hot = eslots.spread_t(eranks[0] + eranks[1], eslots.pick(0))
    send_ref[...] = jnp.dot(hot, feats, preferred_element_type=F32).astype(BF16)
    eslots.pack(0, send_ref, out_ref)
    for t in range(first_ref.shape[1]):
        score = lax.dot_general(feats, gate_ref[t], (((1,), (1,)), ((), ())), preferred_element_type=F32)
        z = [jnp.sum(erank_ref[2 + k] * score, axis=1, keepdims=True) for k in range(2)]
        first_ref[:, t : t + 1] = jax.nn.sigmoid(z[0] - z[1])


def forward_kernel(eslots, *refs):
    n = eslots.arrays
    x_ref, refs = eslots.refs(refs), refs[n:]
    in_refs, out_refs, refs = refs[0:5], refs[5:10], refs[10:]
    y_ref = eslots.refs(refs)
    hidden_ref, rows_ref = refs[n:]
    eslots.unpack(0, x_ref, rows_ref)
    rows = rows_ref[...]
    half = rows.shape[1] // 2
    total = 0.0
    for i in range(4):
        if i < 3:
            pre = jnp.dot(rows, in_refs[i][...], preferred_element_type=F32)
        else:
            pre = jnp.dot(rows[:, :half], in_refs[3][...], preferred_element_type=F32)
            pre = pre + jnp.dot(rows[:, half:], in_refs[4][...], preferred_element_type=F32)
        hidden = jnp.maximum(pre, 0.0).astype(BF16)
        hidden_ref[i] = hidden
        if i < 3:
            total = total + jnp.dot(hidden, out_refs[i][...], preferred_element_type=F32)
        else:
            part = hidden.shape[1] // 2
            total = total + jnp.dot(hidden[:, :part], out_refs[3][...], preferred_element_type=F32)
            total = total + jnp.dot(hidden[:, part:], out_refs[4][...], preferred_element_type=F32)
    rows_ref[...] = total.astype(BF16)
    eslots.pack(0, rows_ref, y_ref)


def backward_kernel(eslots, *refs):
    n = eslots.arrays
    dy_ref, hidden_ref, refs = eslots.refs(refs), refs[n], refs[n + 1 :]
    in_refs, out_refs, refs = refs[0:5], refs[5:10], refs[10:]
    dx_ref = eslots.refs(refs)
    (rows_ref,) = refs[n:]
    eslots.unpack(0, dy_ref, rows_ref)
    rows = rows_ref[...]
    nt = (((1,), (1,)), ((), ()))
    half = rows.shape[1] // 2
    dots = lambda a, refs: [lax.dot_general(a, r[...], nt, preferred_element_type=F32) for r in refs]
    total = low = high = 0.0
    for i in range(4):
        dhidden = jnp.concatenate(dots(rows, out_refs[i : i + 1] if i < 3 else out_refs[3:5]), axis=1)
        dpre = jnp.where(hidden_ref[i].astype(F32) > 0.0, dhidden, 0.0).astype(BF16)
        if i < 3:
            total = total + dots(dpre, in_refs[i : i + 1])[0]
        else:
            low, high = dots(dpre, in_refs[3:5])
    rows_ref[:, :half] = (total[:, :half] + low).astype(BF16)
    rows_ref[:, half:] = (total[:, half:] + high).astype(BF16)
    eslots.pack(0, rows_ref, dx_ref)


def middle_kernel(eslots, *refs):
    n = eslots.arrays
    y_ref, refs = eslots.refs(refs), refs[n:]
    erank_ref, first_ref, label_ref, head_ref, gate_ref, logit_ref, dgate_ref = refs[0:7]
    out_ref = eslots.refs(refs[7:])
    rows_ref, tmp_ref = refs[7 + n :]
    samples, tasks = first_ref.shape
    tmp_ref[...] = jnp.zeros(tmp_ref.shape, F32)
    tmp_ref[0:tasks, 0:samples] = label_ref[...]
    labels = tmp_ref[:, 0:samples].T
    width = eslots.width
    eslots.unpack(0, y_ref, rows_ref)
    rows = rows_ref[...]
    eranks = [erank_ref[k] for k in range(2)]
    picks = eslots.pick(1)
    y0, y1 = [
        jnp.dot(eslots.spread(eranks[k], picks), rows, preferred_element_type=F32) for k in range(2)
    ]
    gap = y0 - y1
    sign = erank_ref[2] - erank_ref[3]
    lane = lax.broadcasted_iota(I32, (samples, LANES), 1)
    logits = jnp.zeros((samples, LANES), F32)
    dy0 = dy1 = dgate = 0.0
    for t in range(tasks):
        g = first_ref[:, t : t + 1]
        rest = 1.0 - g
        comb = g * y0 + rest * y1
        scale = jnp.sqrt(jnp.sum(comb * comb, axis=1, keepdims=True) * (1.0 / width) + norm_eps)
        inv = 1.0 / scale
        normed = comb * inv
        head = head_ref[t : t + 1, :]
        logit = jnp.sum(normed * head, axis=1, keepdims=True)
        logits = jnp.where(lane == t, logit, logits)
        dlogit = jax.nn.sigmoid(logit) - labels[:, t : t + 1]
        drop = dlogit * logit * (1.0 / width)
        dcomb = (dlogit * head - normed * drop) * inv
        dy0 = dy0 + g * dcomb
        dy1 = dy1 + rest * dcomb
        ddelta = jnp.sum(dcomb * gap, axis=1, keepdims=True) * g * rest
        dgate = dgate + jnp.dot(
            ddelta * sign,
            gate_ref[t].astype(F32),
            precision=lax.Precision.HIGHEST,
            preferred_element_type=F32,
        )
    dgate_ref[...] = dgate
    logit_ref[...] = logits.T[0:tasks, :]
    picks = eslots.pick(0)
    send = sum(
        jnp.dot(eslots.spread_t(eranks[k], picks), dy.astype(BF16), preferred_element_type=F32)
        for k, dy in enumerate((dy0, dy1))
    )
    rows_ref[...] = send.astype(BF16)
    eslots.pack(0, rows_ref, out_ref)


def spread_grads_kernel(slots, eslots, *refs):
    dx_ref, refs = eslots.refs(refs), refs[eslots.arrays :]
    erank_ref, dgate_ref, rank_ref, out_ref, rows_ref, grad_ref = refs
    tables = rank_ref.shape[0]
    width, group = slots.width, slots.group
    eslots.unpack(0, dx_ref, rows_ref)
    total = dgate_ref[...] + spread_pair(eslots, erank_ref, rows_ref)
    total = total.astype(BF16)
    picks = slots.pick(0)
    for block in range(slots.blocks):
        grads = 0.0
        for t in range(tables):
            ranks = rank_ref[t, :, block * group : (block + 1) * group]
            grads = grads + jnp.dot(
                slots.spread_t(ranks, picks), total[:, t * width : (t + 1) * width], preferred_element_type=F32
            )
        grad_ref[...] = grads.astype(BF16)
        slots.pack(block, grad_ref, out_ref)


def spread_pair(eslots, erank_ref, rows_ref):
    picks = eslots.pick(1)
    rows = rows_ref[...]
    hot = eslots.spread(erank_ref[0], picks) + eslots.spread(erank_ref[1], picks)
    return jnp.dot(hot, rows, preferred_element_type=F32)


def update_kernel(slots, got_ref, want_ref, table_ref, accum_ref, new_table_ref, new_accum_ref, held_ref, hot_ref, rows_ref, sem):
    copy = pltpu.make_async_copy(table_ref, held_ref, sem)
    copy.start()
    tables, table_rows = accum_ref.shape
    width = slots.width
    grads = 0.0
    for block in range(slots.blocks):
        one_hot_rows(slots, block, want_ref, hot_ref)
        slots.unpack(block, got_ref, rows_ref)
        grads = grads + lax.dot_general(
            rows_ref[...], hot_ref[...], (((0,), (0,)), ((), ())), preferred_element_type=F32
        )
    copy.wait()
    for t in range(tables):
        part = grads[:, t * table_rows : (t + 1) * table_rows]
        total = accum_ref[t : t + 1, :] + jnp.sum(part * part, axis=0, keepdims=True) * (1.0 / width)
        new_accum_ref[t : t + 1, :] = total
        step = part * (learn_rate / jnp.sqrt(total))
        new_table_ref[t] = held_ref[t] - step.T


def gather_weight(w):
    half = w.shape[0] // 2

    def send(x, bit):
        return lax.ppermute(x, "dp", [(i, i ^ bit) for i in range(4)])

    by1 = send(w, 1)
    by2 = send(w, 2)
    low = send(by1[:half], 2)
    high = send(by2[half:], 1)
    return [w, by1, by2, low, high]


def trade(eslots, chunks):
    if not eslots.apart:
        return [lax.all_to_all(chunks[0], "expert", 0, 0, tiled=True)]
    order = sorted(range(1, eslots.peers), key=lambda k: (-(k // 2), k))
    got = {0: chunks[0]}
    for k in order:
        got[k] = lax.ppermute(chunks[k], "expert", [(i, i ^ k) for i in range(eslots.peers)])
    return [got[k] for k in range(eslots.peers)]


def per_device(
    tables, accum, bag_owner, bag_row, bag_len, route, labels, w_in, w_out, gate_w, head
):
    dp_count = lax.axis_size("dp")
    expert_count = lax.axis_size("expert")
    device_count = dp_count * expert_count
    samples = route.shape[0]
    table_count, table_rows, emb = tables.shape
    entries = table_count * table_rows
    lookups = samples * bag_owner.shape[1]
    width = table_count * emb
    tasks = labels.shape[1]
    cap_rows = (5 * lookups + 4 * device_count - 1) // (4 * device_count) + 1
    cap_expert = (2 * samples + expert_count - 1) // expert_count + 1
    slots = Slots(device_count, cap_rows, emb, 32)
    apart = expert_count <= 8
    eslots = Slots(expert_count, cap_expert, width, expert_count, apart)
    shape = jax.ShapeDtypeStruct
    both = ("dp", "expert")
    me = lax.axis_index("expert").astype(I32) if apart else jnp.int32(0)
    me = me.reshape(1)

    ins = gather_weight(w_in[0])
    outs = gather_weight(w_out[0])

    def call(kernel, out_shape, scratch, *args, in_specs=None):
        many = isinstance(out_shape, (list, tuple))
        return pl.pallas_call(
            kernel,
            out_shape=out_shape,
            in_specs=in_specs or vmem(len(args)),
            out_specs=vmem(len(out_shape)) if many else vmem(1)[0],
            scratch_shapes=scratch,
            compiler_params=params(24 if eslots.rows <= 512 else 60),
        )(*args)

    def bind(fn, *static):
        return lambda *refs: fn(*static, *refs)

    square = pltpu.VMEM((LANES, max(LANES, device_count)), F32)
    rank, want, erank = call(
        bind(index_kernel, cap_rows, table_rows),
        [
            shape((table_count, samples, device_count), F32),
            shape((device_count, LANES), I32),
            shape((4, samples, expert_count), F32),
        ],
        [
            pltpu.VMEM((2 * bag_owner.shape[1] + 16, samples), I32),
            square,
            pltpu.SemaphoreType.DMA((4,)),
        ],
        me,
        bag_owner.T,
        bag_row.T,
        bag_len,
        route.T,
        in_specs=[pl.BlockSpec(memory_space=pltpu.SMEM)] + hbm(4),
    )
    gate_t = jnp.swapaxes(gate_w, 1, 2)
    wanted = lax.all_to_all(want, both, 0, 0, tiled=True)
    row_shape = slots.shapes()[0]
    exp_shapes = eslots.shapes()
    hot = pltpu.VMEM((slots.rows, entries), BF16)
    rows = pltpu.VMEM((slots.rows, emb), BF16)
    erows = pltpu.VMEM((eslots.rows, width), BF16)
    served = call(
        bind(gather_kernel, slots),
        row_shape,
        [pltpu.VMEM((entries, emb), F32), hot, rows, pltpu.SemaphoreType.DMA(())],
        wanted,
        tables.reshape(entries, emb),
        in_specs=vmem(1) + hbm(1),
    )
    returned = lax.all_to_all(served, both, 0, 0, tiled=True)
    *outgoing, first = call(
        bind(pool_kernel, slots, eslots),
        exp_shapes + [shape((samples, tasks), F32)],
        [rows, pltpu.VMEM((samples, width), BF16), erows],
        returned,
        rank,
        erank,
        gate_t,
    )
    arrived = trade(eslots, outgoing)
    share = w_in.shape[2]
    *result, hidden = call(
        bind(forward_kernel, eslots),
        exp_shapes + [shape((4, eslots.rows, share), BF16)],
        [erows],
        *arrived,
        *ins,
        *outs,
    )
    back = trade(eslots, result)
    logits, dgate, *grads_out = call(
        bind(middle_kernel, eslots),
        [shape((tasks, samples), F32), shape((samples, width), F32)] + exp_shapes,
        [erows, pltpu.VMEM((LANES, samples), F32)],
        *back,
        erank,
        first,
        labels.T,
        head,
        gate_t,
    )
    arrived_grads = trade(eslots, grads_out)
    dinput = call(bind(backward_kernel, eslots), exp_shapes, [erows], *arrived_grads, hidden, *ins, *outs)
    back_grads = trade(eslots, dinput)
    row_out = call(bind(spread_grads_kernel, slots, eslots), row_shape, [erows, rows], *back_grads, erank, dgate, rank)
    row_in = lax.all_to_all(row_out, both, 0, 0, tiled=True)
    new_tables, new_accum = call(
        bind(update_kernel, slots),
        [shape(tables.shape, F32), shape(accum.shape, F32)],
        [pltpu.VMEM(tables.shape, F32), hot, rows, pltpu.SemaphoreType.DMA(())],
        row_in,
        wanted,
        tables,
        accum,
        in_specs=vmem(2) + hbm(1) + vmem(1),
    )
    return (logits.T, new_tables, new_accum)


def solution(mesh):
    in_specs = (
        P(None, ("dp", "expert"), None),
        P(None, ("dp", "expert")),
        P(("dp", "expert"), None),
        P(("dp", "expert"), None),
        P(None, ("dp", "expert")),
        P(("dp", "expert"), None),
        P(("dp", "expert"), None),
        P("expert", None, "dp"),
        P("expert", "dp", None),
        P(),
        P(),
    )
    out_specs = (
        P(("dp", "expert"), None),
        P(None, ("dp", "expert"), None),
        P(None, ("dp", "expert")),
    )

    return jax.shard_map(per_device, mesh=mesh, in_specs=in_specs, out_specs=out_specs, check_vma=False)
```

```python
import jax
import jax.numpy as jnp
from jax import lax
from jax.experimental import pallas as pl
from jax.experimental.pallas import tpu as pltpu
from jax.sharding import PartitionSpec as P


learn_rate = 0.3
norm_eps = 1e-05
LANES = 128
F32 = jnp.float32
BF16 = jnp.bfloat16
I32 = jnp.int32


def vmem(count):
    return [pl.BlockSpec(memory_space=pltpu.VMEM)] * count


def hbm(count):
    return [pl.BlockSpec(memory_space=pltpu.HBM)] * count


def params(mib):
    return pltpu.CompilerParams(vmem_limit_bytes=mib << 20)


def seq(count, body):
    if count <= 32:
        for i in range(count):
            body(i)
    else:
        lax.fori_loop(0, count, lambda i, c: (body(i), c)[1], 0)


def part(refs, o, a, b):
    return refs[o].at[a:b, :] if isinstance(refs, (list, tuple)) else refs.at[o, a:b, :]


class Slots:
    def __init__(self, peers, cap, width, group, apart=False):
        self.apart = apart
        self.peers, self.width = peers, width
        self.main, self.ext = (cap - 1, 1) if cap % 16 == 1 else (-(-cap // 16) * 16, 0)
        self.lane_blocks = width // LANES
        self.group = min(peers, group)
        self.blocks = peers // self.group
        self.rows = self.group * (self.main + self.ext)
        self.ext_units = -(-self.lane_blocks // 8) * 8 * self.ext
        self.units = self.main * self.lane_blocks + self.ext_units

    @property
    def arrays(self):
        return self.peers if self.apart else 1

    def refs(self, refs):
        return refs[0 : self.peers] if self.apart else refs[0]

    def shapes(self):
        if self.apart:
            return [jax.ShapeDtypeStruct((self.units, LANES), BF16)] * self.peers
        return [jax.ShapeDtypeStruct((self.peers, self.units, LANES), BF16)]

    def pick(self, axis):
        shape = (self.group, self.rows) if axis == 1 else (self.rows, self.group)
        c = lax.broadcasted_iota(I32, shape, axis)
        o = lax.broadcasted_iota(I32, shape, 1 - axis)
        base = o * self.main
        bulk = self.group * self.main
        own = (c >= base) & (c < base + self.main)
        rank = c - base + 1
        if self.ext:
            own = own | (c == bulk + o)
            rank = jnp.where(c < bulk, rank, self.main + 1)
        expand = jnp.where(own, 1.0, 0.0).astype(BF16)
        rank = jnp.sum(jnp.where(own, rank.astype(F32), 0.0), axis=1 - axis, keepdims=True)
        return expand, rank

    def spread(self, ranks, picks):
        expand, rank = picks
        held = jnp.dot(ranks.astype(BF16), expand, preferred_element_type=F32)
        return jnp.where(held == rank, 1.0, 0.0).astype(BF16)

    def spread_t(self, ranks, picks):
        expand, rank = picks
        held = lax.dot_general(
            expand, ranks.astype(BF16), (((1,), (1,)), ((), ())), preferred_element_type=F32
        )
        return jnp.where(held == rank, 1.0, 0.0).astype(BF16)

    def ext_pick(self, j):
        shape = (self.group * self.ext_units, self.group)
        u = lax.broadcasted_iota(I32, shape, 0)
        o = lax.broadcasted_iota(I32, shape, 1)
        return jnp.where(u == o * self.ext_units + j, 1.0, 0.0).astype(BF16)

    def pack(self, block, rows_ref, out_ref):
        self.pack_main(block, rows_ref, out_ref, range(self.group))
        self.pack_ext(block, rows_ref, out_ref)

    def pack_main(self, block, rows_ref, out_ref, peers):
        main, first = self.main, block * self.group

        def one(o):
            start = o * main if isinstance(o, int) else pl.multiple_of(o * main, 16)
            for j in range(self.lane_blocks):
                part(out_ref, first + o, j * main, (j + 1) * main)[...] = rows_ref[
                    pl.ds(start, main), j * LANES : (j + 1) * LANES
                ]

        seq(len(peers), lambda i: one(peers[0] + i))

    def pack_ext(self, block, rows_ref, out_ref):
        main, first = self.main, block * self.group
        if self.ext:
            extra = jnp.zeros((self.group * self.ext_units, LANES), F32)
            tail = rows_ref[self.group * main : self.rows, :]
            for j in range(self.lane_blocks):
                extra = extra + jnp.dot(
                    self.ext_pick(j), tail[:, j * LANES : (j + 1) * LANES], preferred_element_type=F32
                )
            for o in range(self.group):
                part(out_ref, first + o, self.lane_blocks * main, self.units)[...] = extra[
                    o * self.ext_units : (o + 1) * self.ext_units
                ].astype(BF16)

    def unpack(self, block, in_ref, rows_ref):
        main, first = self.main, block * self.group

        def one(o):
            start = o * main if isinstance(o, int) else pl.multiple_of(o * main, 16)
            for j in range(self.lane_blocks):
                rows_ref[pl.ds(start, main), j * LANES : (j + 1) * LANES] = part(
                    in_ref, first + o, j * main, (j + 1) * main
                )[...]

        seq(self.group, one)
        if self.ext:
            extra = [
                part(in_ref, first + o, self.lane_blocks * main, self.units)[...].astype(F32)
                for o in range(self.group)
            ]
            extra = jnp.concatenate(extra, axis=0).astype(BF16)
            for j in range(self.lane_blocks):
                rows_ref[self.group * main : self.rows, j * LANES : (j + 1) * LANES] = (
                    lax.dot_general(
                        self.ext_pick(j),
                        extra,
                        (((0,), (0,)), ((), ())),
                        preferred_element_type=F32,
                    ).astype(BF16)
                )


def one_hot_rows(slots, block, want_ref, hot_ref):
    group, main = slots.group, slots.main
    want = want_ref[block * group : (block + 1) * group, :].astype(F32)
    fill = jnp.zeros((LANES - group, LANES), F32)
    cols = jnp.concatenate([want, fill], axis=0).T
    entry = lax.broadcasted_iota(I32, (main, hot_ref.shape[1]), 1).astype(F32)
    for o in range(group):
        hit = cols[0:main, o : o + 1] == entry
        hot_ref[o * main : (o + 1) * main, :] = jnp.where(hit, 1.0, 0.0).astype(BF16)
    if slots.ext:
        entry = lax.broadcasted_iota(I32, (group, hot_ref.shape[1]), 1).astype(F32)
        hit = want[:, main : main + 1] == entry
        hot_ref[group * main : slots.rows, :] = jnp.where(hit, 1.0, 0.0).astype(BF16)


def plan_spans(columns, tables, owners):
    experts = (columns - tables * owners) // 4
    base = tables * owners
    ranks = [(t * owners, (t + 1) * owners) for t in range(tables)]
    parts = [(base + i * experts, base + (i + 1) * experts) for i in range(4)]
    return ranks, parts[0:2], parts[2:4]


def plan_views(plan_ref, tables, owners):
    plan = plan_ref[...]
    spans = plan_spans(plan.shape[1], tables, owners)
    return [[plan[:, first:last] for first, last in part] for part in spans]


def index_kernel(cap, table_rows, me_ref, owner_ref, row_ref, len_ref, route_ref, plan_ref, want_ref, stage_ref, tmp_ref, sems):
    owners = want_ref.shape[0]
    tables = len_ref.shape[0]
    columns, samples = owner_ref.shape
    ranks, eranks, ehits = plan_spans(plan_ref.shape[1], tables, owners)
    experts = eranks[0][1] - eranks[0][0]

    def keep(span, value):
        plan_ref[:, span[0] : span[1]] = value

    slots = columns // tables
    lines = (0, columns, 2 * columns, 2 * columns + 8)
    counts = (columns, columns, tables, 2)
    copies = [
        pltpu.make_async_copy(ref, stage_ref.at[line : line + count, :], sems.at[i])
        for i, (ref, line, count) in enumerate(zip((owner_ref, row_ref, len_ref, route_ref), lines, counts))
    ]
    for copy in copies:
        copy.start()
    tmp_ref[...] = jnp.zeros(tmp_ref.shape, F32)
    for copy in copies:
        copy.wait()
    for line, count in zip(lines, counts):
        tmp_ref[line : line + count, 0:samples] = stage_ref[line : line + count, :].astype(F32)
    args = tmp_ref[:, 0:samples].T
    peer = lax.broadcasted_iota(I32, (samples, owners), 1).astype(F32)
    entry = jnp.zeros((samples, owners), F32)
    named = []
    for t in range(tables):
        mine = jnp.zeros((samples, owners), F32)
        length = args[:, 2 * columns + t : 2 * columns + t + 1]
        for b in range(slots):
            j = t * slots + b
            live = jnp.where(length > float(b), args[:, j : j + 1], -1.0)
            hit = live == peer
            mine = jnp.where(hit, 1.0, mine)
            entry = jnp.where(hit, args[:, columns + j : columns + j + 1] + float(t * table_rows + 1), entry)
        named.append(mine)
    every = sum(named)
    before = (
        lax.broadcasted_iota(I32, (samples, samples), 0) > lax.broadcasted_iota(I32, (samples, samples), 1)
    )
    before = jnp.where(before, 1.0, 0.0).astype(BF16)
    rank = jnp.dot(before, every.astype(BF16), preferred_element_type=F32) + 1.0
    for t in range(tables):
        keep(ranks[t], named[t] * rank)
    rank = every * rank
    tmp_ref[...] = jnp.zeros(tmp_ref.shape, F32)
    for r in range(cap):
        tmp_ref[r : r + 1, 0:owners] = jnp.sum(
            jnp.where(rank == float(r + 1), entry, 0.0), axis=0, keepdims=True
        )
    want_ref[...] = tmp_ref[...].T[0:owners, :].astype(I32) - 1
    expert = lax.broadcasted_iota(I32, (samples, experts), 1)
    routes = [args[:, 2 * columns + 8 + k : 2 * columns + 9 + k] for k in range(2)]
    for k in range(2):
        keep(ehits[k], jnp.where(routes[k] == expert.astype(F32), 1.0, 0.0))
    expert = (expert ^ me_ref[0]).astype(F32)
    hits = [jnp.where(routes[k] == expert, 1.0, 0.0) for k in range(2)]
    rank = jnp.dot(before, (hits[0] + hits[1]).astype(BF16), preferred_element_type=F32) + 1.0
    for k in range(2):
        keep(eranks[k], hits[k] * rank)


def gather_kernel(slots, want_ref, table_ref, out_ref, held_ref, hot_ref, rows_ref, stage_ref, sems):
    load = pltpu.make_async_copy(table_ref, held_ref, sems.at[0])
    load.start()
    steps = 4 if slots.group % 4 == 0 else 1
    count = slots.group // steps
    bulk = slots.group * slots.main
    stores = []
    for block in range(slots.blocks):
        one_hot_rows(slots, block, want_ref, hot_ref)
        if block == 0:
            load.wait()
            table = held_ref[...].astype(BF16)

        def look_up(first, last):
            rows_ref[first:last, :] = jnp.dot(
                hot_ref[first:last, :], table, preferred_element_type=F32
            ).astype(BF16)

        if slots.ext:
            look_up(bulk, slots.rows)
            slots.pack_ext(block, rows_ref, stage_ref)
        for step in range(steps):
            peers = range(step * count, (step + 1) * count)
            look_up(peers[0] * slots.main, (peers[-1] + 1) * slots.main)
            slots.pack_main(block, rows_ref, stage_ref, peers)
            first = block * slots.group + peers[0]
            store = pltpu.make_async_copy(
                stage_ref.at[first : first + count],
                out_ref.at[first : first + count],
                sems.at[1 + block * steps + step],
            )
            store.start()
            stores.append(store)
    for store in stores:
        store.wait()


def pool_kernel(slots, eslots, tables, got_ref, plan_ref, gate_ref, *refs):
    out_ref = eslots.refs(refs)
    first_ref, rows_ref, feat_ref, send_ref = refs[eslots.arrays :]
    ranks, eranks, ehits = plan_views(plan_ref, tables, slots.peers)
    width = slots.width
    group = slots.group
    picks = slots.pick(1)
    sums = [0.0] * tables
    for block in range(slots.blocks):
        slots.unpack(block, got_ref, rows_ref)
        rows = rows_ref[...]
        for t in range(tables):
            held = ranks[t][:, block * group : (block + 1) * group]
            sums[t] = sums[t] + jnp.dot(slots.spread(held, picks), rows, preferred_element_type=F32)
    for t in range(tables):
        feat_ref[:, t * width : (t + 1) * width] = sums[t].astype(BF16)
    feats = feat_ref[...]
    hot = eslots.spread_t(eranks[0] + eranks[1], eslots.pick(0))
    send_ref[...] = jnp.dot(hot, feats, preferred_element_type=F32).astype(BF16)
    eslots.pack(0, send_ref, out_ref)
    for t in range(first_ref.shape[1]):
        score = lax.dot_general(feats, gate_ref[t], (((1,), (1,)), ((), ())), preferred_element_type=F32)
        z = [jnp.sum(ehits[k] * score, axis=1, keepdims=True) for k in range(2)]
        first_ref[:, t : t + 1] = jax.nn.sigmoid(z[0] - z[1])


def forward_kernel(eslots, *refs):
    n = eslots.arrays
    x_ref, refs = eslots.refs(refs), refs[n:]
    in_refs, out_refs, refs = refs[0:7], refs[7:12], refs[12:]
    total_ref, hidden_ref, rows_ref, in_buf, out_buf, sems = refs
    own = [
        pltpu.make_async_copy(in_refs[0], in_buf, sems.at[0]),
        pltpu.make_async_copy(out_refs[0], out_buf, sems.at[1]),
    ]
    for copy in own:
        copy.start()
    eslots.unpack(0, x_ref, rows_ref)
    rows = rows_ref[...]
    half = rows.shape[1] // 2
    share = hidden_ref.shape[2]
    dot = lambda a, b: jnp.dot(a, b, preferred_element_type=F32)
    total = 0.0
    for i in (1, 2, 3, 0):
        low, high = 2 * i - 1, 2 * i
        if i == 0:
            for copy in own:
                copy.wait()
            pre = dot(rows, in_buf[...])
        else:
            pre = dot(rows[:, :half], in_refs[low][...]) + dot(rows[:, half:], in_refs[high][...])
        hidden = jnp.maximum(pre, 0.0).astype(BF16)
        hidden_ref[i] = hidden
        if i == 0:
            total = total + dot(hidden, out_buf[...])
        elif i < 3:
            total = total + dot(hidden[:, : share // 2], out_refs[low][...])
            total = total + dot(hidden[:, share // 2 :], out_refs[high][...])
    total_ref[...] = total


def finish_kernel(eslots, total_ref, hidden_ref, low_ref, high_ref, *refs):
    y_ref, rows_ref = eslots.refs(refs), refs[eslots.arrays]
    hidden = hidden_ref[3]
    half = hidden.shape[1] // 2
    dot = lambda a, b: jnp.dot(a, b, preferred_element_type=F32)
    total = total_ref[...] + dot(hidden[:, :half], low_ref[...]) + dot(hidden[:, half:], high_ref[...])
    rows_ref[...] = total.astype(BF16)
    eslots.pack(0, rows_ref, y_ref)


def backward_kernel(eslots, *refs):
    n = eslots.arrays
    dy_ref, hidden_ref, refs = eslots.refs(refs), refs[n], refs[n + 1 :]
    in_refs, out_refs, refs = refs[0:7], refs[7:14], refs[14:]
    dx_ref = eslots.refs(refs)
    (rows_ref,) = refs[n:]
    eslots.unpack(0, dy_ref, rows_ref)
    rows = rows_ref[...]
    nt = (((1,), (1,)), ((), ()))
    half = rows.shape[1] // 2
    dot = lambda a, b: lax.dot_general(a, b, nt, preferred_element_type=F32)
    low = high = 0.0
    for i in range(4):
        parts = (0,) if i == 0 else (2 * i - 1, 2 * i)
        dhidden = [dot(rows, out_refs[p][...]) for p in parts]
        dhidden = dhidden[0] if i == 0 else jnp.concatenate(dhidden, axis=1)
        dpre = jnp.where(hidden_ref[i].astype(F32) > 0.0, dhidden, 0.0).astype(BF16)
        if i == 0:
            low, high = low + dot(dpre, in_refs[0][:half, :]), high + dot(dpre, in_refs[0][half:, :])
        else:
            low, high = low + dot(dpre, in_refs[parts[0]][...]), high + dot(dpre, in_refs[parts[1]][...])
    rows_ref[:, :half] = low.astype(BF16)
    rows_ref[:, half:] = high.astype(BF16)
    eslots.pack(0, rows_ref, dx_ref)


def middle_kernel(eslots, tables, owners, *refs):
    n = eslots.arrays
    y_ref, refs = eslots.refs(refs), refs[n:]
    plan_ref, first_ref, label_ref, head_ref, gate_ref, logit_ref, dgate_ref = refs[0:7]
    out_ref = eslots.refs(refs[7:])
    rows_ref, tmp_ref = refs[7 + n :]
    samples, tasks = first_ref.shape
    tmp_ref[...] = jnp.zeros(tmp_ref.shape, F32)
    tmp_ref[0:tasks, 0:samples] = label_ref[...]
    labels = tmp_ref[:, 0:samples].T
    width = eslots.width
    eslots.unpack(0, y_ref, rows_ref)
    rows = rows_ref[...]
    _, eranks, ehits = plan_views(plan_ref, tables, owners)
    picks = eslots.pick(1)
    y0, y1 = [
        jnp.dot(eslots.spread(eranks[k], picks), rows, preferred_element_type=F32) for k in range(2)
    ]
    gap = y0 - y1
    sign = ehits[0] - ehits[1]
    lane = lax.broadcasted_iota(I32, (samples, LANES), 1)
    logits = jnp.zeros((samples, LANES), F32)
    dy0 = dy1 = dgate = 0.0
    for t in range(tasks):
        g = first_ref[:, t : t + 1]
        rest = 1.0 - g
        comb = g * y0 + rest * y1
        scale = jnp.sqrt(jnp.sum(comb * comb, axis=1, keepdims=True) * (1.0 / width) + norm_eps)
        inv = 1.0 / scale
        normed = comb * inv
        head = head_ref[t : t + 1, :]
        logit = jnp.sum(normed * head, axis=1, keepdims=True)
        logits = jnp.where(lane == t, logit, logits)
        dlogit = jax.nn.sigmoid(logit) - labels[:, t : t + 1]
        drop = dlogit * logit * (1.0 / width)
        dcomb = (dlogit * head - normed * drop) * inv
        dy0 = dy0 + g * dcomb
        dy1 = dy1 + rest * dcomb
        ddelta = jnp.sum(dcomb * gap, axis=1, keepdims=True) * g * rest
        dgate = dgate + jnp.dot(
            ddelta * sign,
            gate_ref[t].astype(F32),
            precision=lax.Precision.HIGHEST,
            preferred_element_type=F32,
        )
    dgate_ref[...] = dgate
    logit_ref[...] = logits.T[0:tasks, :]
    picks = eslots.pick(0)
    send = sum(
        jnp.dot(eslots.spread_t(eranks[k], picks), dy.astype(BF16), preferred_element_type=F32)
        for k, dy in enumerate((dy0, dy1))
    )
    rows_ref[...] = send.astype(BF16)
    eslots.pack(0, rows_ref, out_ref)


def spread_grads_kernel(slots, eslots, tables, *refs):
    dx_ref, refs = eslots.refs(refs), refs[eslots.arrays :]
    plan_ref, dgate_ref, out_ref, rows_ref, grad_ref = refs
    ranks, eranks, _ = plan_views(plan_ref, tables, slots.peers)
    width, group = slots.width, slots.group
    eslots.unpack(0, dx_ref, rows_ref)
    total = dgate_ref[...] + spread_pair(eslots, eranks, rows_ref)
    total = total.astype(BF16)
    picks = slots.pick(0)
    for block in range(slots.blocks):
        grads = 0.0
        for t in range(tables):
            held = ranks[t][:, block * group : (block + 1) * group]
            grads = grads + jnp.dot(
                slots.spread_t(held, picks), total[:, t * width : (t + 1) * width], preferred_element_type=F32
            )
        grad_ref[...] = grads.astype(BF16)
        slots.pack(block, grad_ref, out_ref)


def spread_pair(eslots, eranks, rows_ref):
    picks = eslots.pick(1)
    rows = rows_ref[...]
    hot = eslots.spread(eranks[0], picks) + eslots.spread(eranks[1], picks)
    return jnp.dot(hot, rows, preferred_element_type=F32)


def update_kernel(slots, got_ref, want_ref, table_ref, accum_ref, new_table_ref, new_accum_ref, held_ref, hot_ref, rows_ref, sem):
    copy = pltpu.make_async_copy(table_ref, held_ref, sem)
    copy.start()
    tables, table_rows = accum_ref.shape
    width = slots.width
    grads = 0.0
    for block in range(slots.blocks):
        one_hot_rows(slots, block, want_ref, hot_ref)
        slots.unpack(block, got_ref, rows_ref)
        grads = grads + lax.dot_general(
            rows_ref[...], hot_ref[...], (((0,), (0,)), ((), ())), preferred_element_type=F32
        )
    copy.wait()
    for t in range(tables):
        part = grads[:, t * table_rows : (t + 1) * table_rows]
        total = accum_ref[t : t + 1, :] + jnp.sum(part * part, axis=0, keepdims=True) * (1.0 / width)
        new_accum_ref[t : t + 1, :] = total
        step = part * (learn_rate / jnp.sqrt(total))
        new_table_ref[t] = held_ref[t] - step.T


def gather_weight(w, later):
    half = w.shape[0] // 2

    def send(x, bit):
        return lax.ppermute(x, "dp", [(i, i ^ bit) for i in range(4)])

    low, high = w[:half], lax.optimization_barrier((w, later))[0][half:]
    low1, low2 = send(low, 1), send(low, 2)
    high1, high2 = send(high, 1), send(high, 2)
    return [w, low1, high1, low2, high2, send(low1, 2), send(high2, 1)]


def trade(eslots, chunks):
    if not eslots.apart:
        return [lax.all_to_all(chunks[0], "expert", 0, 0, tiled=True)]
    order = sorted(range(1, eslots.peers), key=lambda k: (-(k // 2), k))
    got = {0: chunks[0]}
    for k in order:
        got[k] = lax.ppermute(chunks[k], "expert", [(i, i ^ k) for i in range(eslots.peers)])
    return [got[k] for k in range(eslots.peers)]


def per_device(
    tables, accum, bag_owner, bag_row, bag_len, route, labels, w_in, w_out, gate_w, head
):
    dp_count = lax.axis_size("dp")
    expert_count = lax.axis_size("expert")
    device_count = dp_count * expert_count
    samples = route.shape[0]
    table_count, table_rows, emb = tables.shape
    entries = table_count * table_rows
    lookups = samples * bag_owner.shape[1]
    width = table_count * emb
    tasks = labels.shape[1]
    cap_rows = (5 * lookups + 4 * device_count - 1) // (4 * device_count) + 1
    cap_expert = (2 * samples + expert_count - 1) // expert_count + 1
    slots = Slots(device_count, cap_rows, emb, 32)
    apart = expert_count <= 8
    eslots = Slots(expert_count, cap_expert, width, expert_count, apart)
    shape = jax.ShapeDtypeStruct
    both = ("dp", "expert")
    me = lax.axis_index("expert").astype(I32) if apart else jnp.int32(0)
    me = me.reshape(1)

    def off(x):
        return pltpu.with_memory_space_constraint(x, pltpu.HBM)

    def call(kernel, out_shape, scratch, *args, in_specs=None, out_specs=None):
        many = isinstance(out_shape, (list, tuple))
        return pl.pallas_call(
            kernel,
            out_shape=out_shape,
            in_specs=in_specs or vmem(len(args)),
            out_specs=out_specs or (vmem(len(out_shape)) if many else vmem(1)[0]),
            scratch_shapes=scratch,
            compiler_params=params(24 if eslots.rows <= 512 else 60),
        )(*args)

    def bind(fn, *static):
        return lambda *refs: fn(*static, *refs)

    square = pltpu.VMEM((LANES, max(LANES, device_count)), F32)
    plan, want = call(
        bind(index_kernel, cap_rows, table_rows),
        [
            shape((samples, table_count * device_count + 4 * expert_count), F32),
            shape((device_count, LANES), I32),
        ],
        [
            pltpu.VMEM((2 * bag_owner.shape[1] + 16, samples), I32),
            square,
            pltpu.SemaphoreType.DMA((4,)),
        ],
        me,
        off(bag_owner.T),
        off(bag_row.T),
        off(bag_len),
        off(route.T),
        in_specs=[pl.BlockSpec(memory_space=pltpu.SMEM)] + hbm(4),
    )
    ins = gather_weight(w_in[0], plan)
    outs = gather_weight(w_out[0], plan)
    gate_t = jnp.swapaxes(gate_w, 1, 2)
    wanted = lax.all_to_all(want, both, 0, 0, tiled=True)
    row_shape = slots.shapes()[0]
    exp_shapes = eslots.shapes()
    n = len(exp_shapes)
    hot = pltpu.VMEM((slots.rows, entries), BF16)
    rows = pltpu.VMEM((slots.rows, emb), BF16)
    erows = pltpu.VMEM((eslots.rows, width), BF16)
    served = call(
        bind(gather_kernel, slots),
        pltpu.HBM(row_shape.shape, BF16),
        [
            pltpu.VMEM((entries, emb), F32),
            hot,
            rows,
            pltpu.VMEM(row_shape.shape, BF16),
            pltpu.SemaphoreType.DMA((1 + 4 * slots.blocks,)),
        ],
        wanted,
        off(tables.reshape(entries, emb)),
        in_specs=vmem(1) + hbm(1),
        out_specs=hbm(1)[0],
    )
    returned = lax.all_to_all(served, both, 0, 0, tiled=True)
    *outgoing, first = call(
        bind(pool_kernel, slots, eslots, table_count),
        exp_shapes + [shape((samples, tasks), F32)],
        [rows, pltpu.VMEM((samples, width), BF16), erows],
        returned,
        plan,
        gate_t,
    )
    arrived = trade(eslots, outgoing)
    share = w_in.shape[2]
    own = [
        pltpu.VMEM((width, share), BF16),
        pltpu.VMEM((share, width), BF16),
        pltpu.SemaphoreType.DMA((2,)),
    ]
    total, hidden = call(
        bind(forward_kernel, eslots),
        [shape((eslots.rows, width), F32), shape((4, eslots.rows, share), BF16)],
        [erows] + own,
        *arrived,
        off(ins[0]),
        *ins[1:],
        off(outs[0]),
        *outs[1:5],
        in_specs=vmem(n) + hbm(1) + vmem(6) + hbm(1) + vmem(4),
    )
    result = call(bind(finish_kernel, eslots), exp_shapes, [erows], total, hidden, *outs[5:7])
    back = trade(eslots, result)
    logits, dgate, *grads_out = call(
        bind(middle_kernel, eslots, table_count, device_count),
        [shape((tasks, samples), F32), shape((samples, width), F32)] + exp_shapes,
        [erows, pltpu.VMEM((LANES, samples), F32)],
        *back,
        plan,
        first,
        labels.T,
        head,
        gate_t,
    )
    arrived_grads = trade(eslots, grads_out)
    dinput = call(
        bind(backward_kernel, eslots), exp_shapes, [erows], *arrived_grads, hidden, *ins, *outs
    )
    back_grads = trade(eslots, dinput)
    row_out = call(
        bind(spread_grads_kernel, slots, eslots, table_count),
        row_shape,
        [erows, rows],
        *back_grads,
        plan,
        dgate,
    )
    row_in = lax.all_to_all(row_out, both, 0, 0, tiled=True)
    new_tables, new_accum = call(
        bind(update_kernel, slots),
        [shape(tables.shape, F32), shape(accum.shape, F32)],
        [pltpu.VMEM(tables.shape, F32), hot, rows, pltpu.SemaphoreType.DMA(())],
        row_in,
        wanted,
        off(tables),
        accum,
        in_specs=vmem(2) + hbm(1) + vmem(1),
    )
    return (logits.T, new_tables, new_accum)


def solution(mesh):
    in_specs = (
        P(None, ("dp", "expert"), None),
        P(None, ("dp", "expert")),
        P(("dp", "expert"), None),
        P(("dp", "expert"), None),
        P(None, ("dp", "expert")),
        P(("dp", "expert"), None),
        P(("dp", "expert"), None),
        P("expert", None, "dp"),
        P("expert", "dp", None),
        P(),
        P(),
    )
    out_specs = (
        P(("dp", "expert"), None),
        P(None, ("dp", "expert"), None),
        P(None, ("dp", "expert")),
    )

    return jax.shard_map(per_device, mesh=mesh, in_specs=in_specs, out_specs=out_specs, check_vma=False)
```

```python
import jax
import jax.numpy as jnp
from jax import lax
from jax.experimental import pallas as pl
from jax.experimental.pallas import tpu as pltpu
from jax.sharding import PartitionSpec as P


learn_rate = 0.3
norm_eps = 1e-05
LANES = 128
F32 = jnp.float32
BF16 = jnp.bfloat16
I32 = jnp.int32


GRANTS = {"gather": 16, "update": 16, "pool": 12, "prepare": 12}


def vmem(count):
    return [pl.BlockSpec(memory_space=pltpu.VMEM)] * count


def hbm(count):
    return [pl.BlockSpec(memory_space=pltpu.HBM)] * count


def params(mib):
    return pltpu.CompilerParams(vmem_limit_bytes=mib << 20)


def seq(count, body):
    if count <= 32:
        for i in range(count):
            body(i)
    else:
        lax.fori_loop(0, count, lambda i, c: (body(i), c)[1], 0)


def part(refs, o, a, b):
    return refs[o].at[a:b, :] if isinstance(refs, (list, tuple)) else refs.at[o, a:b, :]


class Slots:
    def __init__(self, peers, cap, width, group, apart=False):
        self.apart = apart
        self.peers, self.width = peers, width
        self.main, self.ext = (cap - 1, 1) if cap % 16 == 1 else (-(-cap // 16) * 16, 0)
        self.lane_blocks = width // LANES
        self.group = min(peers, group)
        self.blocks = peers // self.group
        self.rows = self.group * (self.main + self.ext)
        self.ext_units = -(-self.lane_blocks // 8) * 8 * self.ext
        self.units = self.main * self.lane_blocks + self.ext_units

    @property
    def arrays(self):
        return self.peers if self.apart else 1

    def refs(self, refs):
        return refs[0 : self.peers] if self.apart else refs[0]

    def shapes(self):
        if self.apart:
            return [jax.ShapeDtypeStruct((self.units, LANES), BF16)] * self.peers
        return [jax.ShapeDtypeStruct((self.peers, self.units, LANES), BF16)]

    def pick(self, axis):
        shape = (self.group, self.rows) if axis == 1 else (self.rows, self.group)
        c = lax.broadcasted_iota(I32, shape, axis)
        o = lax.broadcasted_iota(I32, shape, 1 - axis)
        base = o * self.main
        bulk = self.group * self.main
        own = (c >= base) & (c < base + self.main)
        rank = c - base + 1
        if self.ext:
            own = own | (c == bulk + o)
            rank = jnp.where(c < bulk, rank, self.main + 1)
        expand = jnp.where(own, 1.0, 0.0).astype(BF16)
        rank = jnp.sum(jnp.where(own, rank.astype(F32), 0.0), axis=1 - axis, keepdims=True)
        return expand, rank

    def spread(self, ranks, picks):
        expand, rank = picks
        held = jnp.dot(ranks.astype(BF16), expand, preferred_element_type=F32)
        return jnp.where(held == rank, 1.0, 0.0).astype(BF16)

    def spread_t(self, ranks, picks):
        expand, rank = picks
        held = lax.dot_general(
            expand, ranks.astype(BF16), (((1,), (1,)), ((), ())), preferred_element_type=F32
        )
        return jnp.where(held == rank, 1.0, 0.0).astype(BF16)

    def ext_pick(self, j):
        shape = (self.group * self.ext_units, self.group)
        u = lax.broadcasted_iota(I32, shape, 0)
        o = lax.broadcasted_iota(I32, shape, 1)
        return jnp.where(u == o * self.ext_units + j, 1.0, 0.0).astype(BF16)

    def pack(self, block, rows_ref, out_ref):
        self.pack_main(block, rows_ref, out_ref, range(self.group))
        self.pack_ext(block, rows_ref, out_ref)

    def pack_main(self, block, rows_ref, out_ref, peers):
        main, first = self.main, block * self.group

        def one(o):
            start = o * main if isinstance(o, int) else pl.multiple_of(o * main, 16)
            for j in range(self.lane_blocks):
                part(out_ref, first + o, j * main, (j + 1) * main)[...] = rows_ref[
                    pl.ds(start, main), j * LANES : (j + 1) * LANES
                ]

        seq(len(peers), lambda i: one(peers[0] + i))

    def pack_ext(self, block, rows_ref, out_ref):
        main, first = self.main, block * self.group
        if self.ext:
            extra = jnp.zeros((self.group * self.ext_units, LANES), F32)
            tail = rows_ref[self.group * main : self.rows, :]
            for j in range(self.lane_blocks):
                extra = extra + jnp.dot(
                    self.ext_pick(j), tail[:, j * LANES : (j + 1) * LANES], preferred_element_type=F32
                )
            for o in range(self.group):
                part(out_ref, first + o, self.lane_blocks * main, self.units)[...] = extra[
                    o * self.ext_units : (o + 1) * self.ext_units
                ].astype(BF16)

    def unpack(self, block, in_ref, rows_ref):
        main, first = self.main, block * self.group

        def one(o):
            start = o * main if isinstance(o, int) else pl.multiple_of(o * main, 16)
            for j in range(self.lane_blocks):
                rows_ref[pl.ds(start, main), j * LANES : (j + 1) * LANES] = part(
                    in_ref, first + o, j * main, (j + 1) * main
                )[...]

        seq(self.group, one)
        if self.ext:
            extra = [
                part(in_ref, first + o, self.lane_blocks * main, self.units)[...].astype(F32)
                for o in range(self.group)
            ]
            extra = jnp.concatenate(extra, axis=0).astype(BF16)
            for j in range(self.lane_blocks):
                rows_ref[self.group * main : self.rows, j * LANES : (j + 1) * LANES] = (
                    lax.dot_general(
                        self.ext_pick(j),
                        extra,
                        (((0,), (0,)), ((), ())),
                        preferred_element_type=F32,
                    ).astype(BF16)
                )


def prepare_kernel(slots, tables, plan_ref, tall_ref):
    ranks, _, _ = plan_views(plan_ref, tables, slots.peers)
    samples = plan_ref.shape[0]
    group = slots.group
    picks = slots.pick(0)
    for block in range(slots.blocks):
        for t in range(tables):
            held = ranks[t][:, block * group : (block + 1) * group]
            tall_ref[block, :, t * samples : (t + 1) * samples] = slots.spread_t(held, picks)


def one_hot_rows(slots, block, want_ref, hot_ref):
    group, main = slots.group, slots.main
    want = want_ref[block * group : (block + 1) * group, :].astype(F32)
    fill = jnp.zeros((LANES - group, LANES), F32)
    cols = jnp.concatenate([want, fill], axis=0).T
    entry = lax.broadcasted_iota(I32, (main, hot_ref.shape[1]), 1).astype(F32)
    for o in range(group):
        hit = cols[0:main, o : o + 1] == entry
        hot_ref[o * main : (o + 1) * main, :] = jnp.where(hit, 1.0, 0.0).astype(BF16)
    if slots.ext:
        entry = lax.broadcasted_iota(I32, (group, hot_ref.shape[1]), 1).astype(F32)
        hit = want[:, main : main + 1] == entry
        hot_ref[group * main : slots.rows, :] = jnp.where(hit, 1.0, 0.0).astype(BF16)


def plan_spans(columns, tables, owners):
    experts = (columns - tables * owners) // 4
    base = tables * owners
    ranks = [(t * owners, (t + 1) * owners) for t in range(tables)]
    parts = [(base + i * experts, base + (i + 1) * experts) for i in range(4)]
    return ranks, parts[0:2], parts[2:4]


def plan_views(plan_ref, tables, owners):
    plan = plan_ref[...]
    spans = plan_spans(plan.shape[1], tables, owners)
    return [[plan[:, first:last] for first, last in part] for part in spans]


def index_kernel(cap, table_rows, me_ref, owner_ref, row_ref, len_ref, route_ref, plan_ref, want_ref, stage_ref, tmp_ref, sems):
    owners = want_ref.shape[0]
    tables = len_ref.shape[0]
    columns, samples = owner_ref.shape
    ranks, eranks, ehits = plan_spans(plan_ref.shape[1], tables, owners)
    experts = eranks[0][1] - eranks[0][0]

    def keep(span, value):
        plan_ref[:, span[0] : span[1]] = value

    slots = columns // tables
    lines = (0, columns, 2 * columns, 2 * columns + 8)
    counts = (columns, columns, tables, 2)
    copies = [
        pltpu.make_async_copy(ref, stage_ref.at[line : line + count, :], sems.at[i])
        for i, (ref, line, count) in enumerate(zip((owner_ref, row_ref, len_ref, route_ref), lines, counts))
    ]
    for copy in copies:
        copy.start()
    tmp_ref[...] = jnp.zeros(tmp_ref.shape, F32)
    for copy in copies:
        copy.wait()
    for line, count in zip(lines, counts):
        tmp_ref[line : line + count, 0:samples] = stage_ref[line : line + count, :].astype(F32)
    args = tmp_ref[:, 0:samples].T
    peer = lax.broadcasted_iota(I32, (samples, owners), 1).astype(F32)
    entry = jnp.zeros((samples, owners), F32)
    named = []
    for t in range(tables):
        mine = jnp.zeros((samples, owners), F32)
        length = args[:, 2 * columns + t : 2 * columns + t + 1]
        for b in range(slots):
            j = t * slots + b
            live = jnp.where(length > float(b), args[:, j : j + 1], -1.0)
            hit = live == peer
            mine = jnp.where(hit, 1.0, mine)
            entry = jnp.where(hit, args[:, columns + j : columns + j + 1] + float(t * table_rows + 1), entry)
        named.append(mine)
    every = sum(named)
    before = (
        lax.broadcasted_iota(I32, (samples, samples), 0) > lax.broadcasted_iota(I32, (samples, samples), 1)
    )
    before = jnp.where(before, 1.0, 0.0).astype(BF16)
    rank = jnp.dot(before, every.astype(BF16), preferred_element_type=F32) + 1.0
    for t in range(tables):
        keep(ranks[t], named[t] * rank)
    rank = every * rank
    tmp_ref[...] = jnp.zeros(tmp_ref.shape, F32)
    for r in range(cap):
        tmp_ref[r : r + 1, 0:owners] = jnp.sum(
            jnp.where(rank == float(r + 1), entry, 0.0), axis=0, keepdims=True
        )
    want_ref[...] = tmp_ref[...].T[0:owners, :].astype(I32) - 1
    expert = lax.broadcasted_iota(I32, (samples, experts), 1)
    routes = [args[:, 2 * columns + 8 + k : 2 * columns + 9 + k] for k in range(2)]
    for k in range(2):
        keep(ehits[k], jnp.where(routes[k] == expert.astype(F32), 1.0, 0.0))
    expert = (expert ^ me_ref[0]).astype(F32)
    hits = [jnp.where(routes[k] == expert, 1.0, 0.0) for k in range(2)]
    rank = jnp.dot(before, (hits[0] + hits[1]).astype(BF16), preferred_element_type=F32) + 1.0
    for k in range(2):
        keep(eranks[k], hits[k] * rank)


def gather_kernel(slots, want_ref, table_ref, out_ref, held_ref, hot_ref, rows_ref, stage_ref, sems):
    load = pltpu.make_async_copy(table_ref, held_ref, sems.at[0])
    load.start()
    steps = 4 if slots.group % 4 == 0 else 1
    count = slots.group // steps
    bulk = slots.group * slots.main
    stores = []
    for block in range(slots.blocks):
        one_hot_rows(slots, block, want_ref, hot_ref)
        if block == 0:
            load.wait()
            table = held_ref[...].astype(BF16)

        def look_up(first, last):
            rows_ref[first:last, :] = jnp.dot(
                hot_ref[first:last, :], table, preferred_element_type=F32
            ).astype(BF16)

        if slots.ext:
            look_up(bulk, slots.rows)
            slots.pack_ext(block, rows_ref, stage_ref)
        for step in range(steps):
            peers = range(step * count, (step + 1) * count)
            look_up(peers[0] * slots.main, (peers[-1] + 1) * slots.main)
            slots.pack_main(block, rows_ref, stage_ref, peers)
            first = block * slots.group + peers[0]
            store = pltpu.make_async_copy(
                stage_ref.at[first : first + count],
                out_ref.at[first : first + count],
                sems.at[1 + block * steps + step],
            )
            store.start()
            stores.append(store)
    for store in stores:
        store.wait()


def pool_kernel(slots, eslots, tables, got_ref, plan_ref, gate_ref, *refs):
    out_ref = eslots.refs(refs)
    first_ref, rows_ref, feat_ref, send_ref = refs[eslots.arrays :]
    ranks, eranks, ehits = plan_views(plan_ref, tables, slots.peers)
    width = slots.width
    group = slots.group
    picks = slots.pick(1)
    sums = [0.0] * tables
    for block in range(slots.blocks):
        slots.unpack(block, got_ref, rows_ref)
        rows = rows_ref[...]
        for t in range(tables):
            held = ranks[t][:, block * group : (block + 1) * group]
            sums[t] = sums[t] + jnp.dot(slots.spread(held, picks), rows, preferred_element_type=F32)
    for t in range(tables):
        feat_ref[:, t * width : (t + 1) * width] = sums[t].astype(BF16)
    feats = feat_ref[...]
    hot = eslots.spread_t(eranks[0] + eranks[1], eslots.pick(0))
    send_ref[...] = jnp.dot(hot, feats, preferred_element_type=F32).astype(BF16)
    eslots.pack(0, send_ref, out_ref)
    for t in range(first_ref.shape[1]):
        score = lax.dot_general(feats, gate_ref[t], (((1,), (1,)), ((), ())), preferred_element_type=F32)
        z = [jnp.sum(ehits[k] * score, axis=1, keepdims=True) for k in range(2)]
        first_ref[:, t : t + 1] = jax.nn.sigmoid(z[0] - z[1])


def forward_kernel(eslots, *refs):
    n = eslots.arrays
    x_ref, refs = eslots.refs(refs), refs[n:]
    in_refs, out_refs, refs = refs[0:7], refs[7:12], refs[12:]
    total_ref, last_ref, *hidden_refs, rows_ref, in_buf, out_buf, sems = refs
    own = [
        pltpu.make_async_copy(in_refs[0], in_buf, sems.at[0]),
        pltpu.make_async_copy(out_refs[0], out_buf, sems.at[1]),
    ]
    for copy in own:
        copy.start()
    eslots.unpack(0, x_ref, rows_ref)
    rows = rows_ref[...]
    half = rows.shape[1] // 2
    share = last_ref.shape[1]
    dot = lambda a, b: jnp.dot(a, b, preferred_element_type=F32)
    total = 0.0
    for i in (1, 2, 3, 0):
        low, high = 2 * i - 1, 2 * i
        if i == 0:
            for copy in own:
                copy.wait()
            pre = dot(rows, in_buf[...])
        else:
            pre = dot(rows[:, :half], in_refs[low][...]) + dot(rows[:, half:], in_refs[high][...])
        pre = jnp.maximum(pre, 0.0)
        hidden = pre.astype(BF16)
        if i == 3:
            last_ref[...] = hidden
        count = eslots.peers // len(hidden_refs)
        bulk, extra = count * eslots.main, count * eslots.ext
        for part, ref in enumerate(hidden_refs):
            ref[i, 0:bulk, :] = hidden[part * bulk : (part + 1) * bulk]
            if extra:
                first = eslots.peers * eslots.main
                tail = pre[first : eslots.rows]
                ref[i, bulk : bulk + extra, :] = tail[part * extra : (part + 1) * extra].astype(BF16)
        if i == 0:
            total = total + dot(hidden, out_buf[...])
        elif i < 3:
            total = total + dot(hidden[:, : share // 2], out_refs[low][...])
            total = total + dot(hidden[:, share // 2 :], out_refs[high][...])
    total_ref[...] = total


def finish_kernel(eslots, total_ref, last_ref, low_ref, high_ref, *refs):
    y_ref, rows_ref = eslots.refs(refs), refs[eslots.arrays]
    hidden = last_ref[...]
    half = hidden.shape[1] // 2
    dot = lambda a, b: jnp.dot(a, b, preferred_element_type=F32)
    total = total_ref[...] + dot(hidden[:, :half], low_ref[...]) + dot(hidden[:, half:], high_ref[...])
    rows_ref[...] = total.astype(BF16)
    eslots.pack(0, rows_ref, y_ref)


def backward_kernel(eslots, *refs):
    n = eslots.arrays
    dy_ref, hidden_ref, refs = eslots.refs(refs), refs[n], refs[n + 1 :]
    in_refs, out_refs, refs = refs[0:7], refs[7:14], refs[14:]
    dx_ref = eslots.refs(refs)
    (rows_ref,) = refs[n:]
    eslots.unpack(0, dy_ref, rows_ref)
    rows = rows_ref[...]
    nt = (((1,), (1,)), ((), ()))
    half = rows.shape[1] // 2
    dot = lambda a, b: lax.dot_general(a, b, nt, preferred_element_type=F32)
    low = high = 0.0
    for i in range(4):
        parts = (0,) if i == 0 else (2 * i - 1, 2 * i)
        dhidden = [dot(rows, out_refs[p][...]) for p in parts]
        dhidden = dhidden[0] if i == 0 else jnp.concatenate(dhidden, axis=1)
        dpre = jnp.where(hidden_ref[i].astype(F32) > 0.0, dhidden, 0.0).astype(BF16)
        if i == 0:
            low, high = low + dot(dpre, in_refs[0][:half, :]), high + dot(dpre, in_refs[0][half:, :])
        else:
            low, high = low + dot(dpre, in_refs[parts[0]][...]), high + dot(dpre, in_refs[parts[1]][...])
    rows_ref[:, :half] = low.astype(BF16)
    rows_ref[:, half:] = high.astype(BF16)
    eslots.pack(0, rows_ref, dx_ref)


def hold_kernel(*refs):
    count = len(refs) // 2
    copies = [
        pltpu.make_async_copy(refs[i], refs[count + i], refs[2 * count].at[i]) for i in range(count)
    ]
    for copy in copies:
        copy.start()
    for copy in copies:
        copy.wait()


def middle_kernel(eslots, tables, owners, *refs):
    n = eslots.arrays
    y_ref, refs = eslots.refs(refs), refs[n:]
    plan_ref, first_ref, label_ref, head_ref, gate_ref, logit_ref, dgate_ref = refs[0:7]
    out_ref = eslots.refs(refs[7:])
    rows_ref, tmp_ref = refs[7 + n :]
    samples, tasks = first_ref.shape
    tmp_ref[...] = jnp.zeros(tmp_ref.shape, F32)
    tmp_ref[0:tasks, 0:samples] = label_ref[...]
    labels = tmp_ref[:, 0:samples].T
    width = eslots.width
    eslots.unpack(0, y_ref, rows_ref)
    rows = rows_ref[...]
    _, eranks, ehits = plan_views(plan_ref, tables, owners)
    picks = eslots.pick(1)
    y0, y1 = [
        jnp.dot(eslots.spread(eranks[k], picks), rows, preferred_element_type=F32) for k in range(2)
    ]
    gap = y0 - y1
    sign = ehits[0] - ehits[1]
    lane = lax.broadcasted_iota(I32, (samples, LANES), 1)
    logits = jnp.zeros((samples, LANES), F32)
    dy0 = dy1 = dgate = 0.0
    for t in range(tasks):
        g = first_ref[:, t : t + 1]
        rest = 1.0 - g
        comb = g * y0 + rest * y1
        scale = jnp.sqrt(jnp.sum(comb * comb, axis=1, keepdims=True) * (1.0 / width) + norm_eps)
        inv = 1.0 / scale
        normed = comb * inv
        head = head_ref[t : t + 1, :]
        logit = jnp.sum(normed * head, axis=1, keepdims=True)
        logits = jnp.where(lane == t, logit, logits)
        dlogit = jax.nn.sigmoid(logit) - labels[:, t : t + 1]
        drop = dlogit * logit * (1.0 / width)
        dcomb = (dlogit * head - normed * drop) * inv
        dy0 = dy0 + g * dcomb
        dy1 = dy1 + rest * dcomb
        ddelta = jnp.sum(dcomb * gap, axis=1, keepdims=True) * g * rest
        dgate = dgate + jnp.dot(
            ddelta * sign,
            gate_ref[t].astype(F32),
            precision=lax.Precision.HIGHEST,
            preferred_element_type=F32,
        )
    dgate_ref[...] = dgate
    logit_ref[...] = logits.T[0:tasks, :]
    picks = eslots.pick(0)
    send = sum(
        jnp.dot(eslots.spread_t(eranks[k], picks), dy.astype(BF16), preferred_element_type=F32)
        for k, dy in enumerate((dy0, dy1))
    )
    rows_ref[...] = send.astype(BF16)
    eslots.pack(0, rows_ref, out_ref)


def spread_grads_kernel(slots, eslots, tables, *refs):
    dx_ref, refs = eslots.refs(refs), refs[eslots.arrays :]
    plan_ref, dgate_ref, tall_ref, out_ref, rows_ref, grad_ref = refs
    _, eranks, _ = plan_views(plan_ref, tables, slots.peers)
    width = slots.width
    eslots.unpack(0, dx_ref, rows_ref)
    total = dgate_ref[...] + spread_pair(eslots, eranks, rows_ref)
    total = total.astype(BF16)
    stacked = jnp.concatenate([total[:, t * width : (t + 1) * width] for t in range(tables)], axis=0)
    for block in range(slots.blocks):
        grad_ref[...] = jnp.dot(tall_ref[block], stacked, preferred_element_type=F32).astype(BF16)
        slots.pack(block, grad_ref, out_ref)


def spread_pair(eslots, eranks, rows_ref):
    picks = eslots.pick(1)
    rows = rows_ref[...]
    hot = eslots.spread(eranks[0], picks) + eslots.spread(eranks[1], picks)
    return jnp.dot(hot, rows, preferred_element_type=F32)


def update_kernel(slots, got_ref, want_ref, table_ref, accum_ref, new_table_ref, new_accum_ref, held_ref, hot_ref, rows_ref, sem):
    copy = pltpu.make_async_copy(table_ref, held_ref, sem)
    copy.start()
    tables, table_rows = accum_ref.shape
    width = slots.width
    grads = 0.0
    for block in range(slots.blocks):
        one_hot_rows(slots, block, want_ref, hot_ref)
        slots.unpack(block, got_ref, rows_ref)
        grads = grads + lax.dot_general(
            rows_ref[...], hot_ref[...], (((0,), (0,)), ((), ())), preferred_element_type=F32
        )
    copy.wait()
    for t in range(tables):
        part = grads[:, t * table_rows : (t + 1) * table_rows]
        total = accum_ref[t : t + 1, :] + jnp.sum(part * part, axis=0, keepdims=True) * (1.0 / width)
        new_accum_ref[t : t + 1, :] = total
        step = part * (learn_rate / jnp.sqrt(total))
        new_table_ref[t] = held_ref[t] - step.T


def cut_kernel(w_ref, out_ref, sem):
    copy = pltpu.make_async_copy(w_ref.at[0 : out_ref.shape[0]], out_ref, sem)
    copy.start()
    copy.wait()


def gather_weight(w, low, later):
    half = w.shape[0] // 2

    def send(x, bit):
        return lax.ppermute(x, "dp", [(i, i ^ bit) for i in range(4)])

    high = lax.optimization_barrier((w, later))[0][half:]
    low1, low2 = send(low, 1), send(low, 2)
    high1, high2 = send(high, 1), send(high, 2)
    return [w, low1, high1, low2, high2, send(low1, 2), send(high2, 1)]


def trade_one(eslots, chunk, k):
    return lax.ppermute(chunk, "expert", [(i, i ^ k) for i in range(eslots.peers)])


def trade(eslots, chunks):
    if not eslots.apart:
        return [lax.all_to_all(chunks[0], "expert", 0, 0, tiled=True)]
    got = {0: chunks[0]}
    for k in sorted(range(1, eslots.peers), key=lambda k: (-(k // 2), k)):
        got[k] = trade_one(eslots, chunks[k], k)
    return [got[k] for k in range(eslots.peers)]


def trade_near(eslots, chunks):
    return [chunks[0]] + [trade_one(eslots, x, k + 1) for k, x in enumerate(chunks[1:])]


def per_device(
    tables, accum, bag_owner, bag_row, bag_len, route, labels, w_in, w_out, gate_w, head
):
    dp_count = lax.axis_size("dp")
    expert_count = lax.axis_size("expert")
    device_count = dp_count * expert_count
    samples = route.shape[0]
    table_count, table_rows, emb = tables.shape
    entries = table_count * table_rows
    lookups = samples * bag_owner.shape[1]
    width = table_count * emb
    tasks = labels.shape[1]
    cap_rows = (5 * lookups + 4 * device_count - 1) // (4 * device_count) + 1
    cap_expert = (2 * samples + expert_count - 1) // expert_count + 1
    slots = Slots(device_count, cap_rows, emb, 32)
    apart = expert_count <= 8
    eslots = Slots(expert_count, cap_expert, width, expert_count, apart)
    shape = jax.ShapeDtypeStruct
    both = ("dp", "expert")
    me = lax.axis_index("expert").astype(I32) if apart else jnp.int32(0)
    me = me.reshape(1)

    def off(x):
        return pltpu.with_memory_space_constraint(x, pltpu.HBM)

    def call(name, kernel, out_shape, scratch, *args, in_specs=None, out_specs=None):
        many = isinstance(out_shape, (list, tuple))
        return pl.pallas_call(
            kernel,
            out_shape=out_shape,
            in_specs=in_specs or vmem(len(args)),
            out_specs=out_specs or (vmem(len(out_shape)) if many else vmem(1)[0]),
            scratch_shapes=scratch,
            compiler_params=params(GRANTS.get(name, 8) if eslots.rows <= 512 else 60),
        )(*args)

    def bind(fn, *static):
        return lambda *refs: fn(*static, *refs)

    square = pltpu.VMEM((LANES, max(LANES, device_count)), F32)
    plan, want = call(
        "index",
        bind(index_kernel, cap_rows, table_rows),
        [
            shape((samples, table_count * device_count + 4 * expert_count), F32),
            shape((device_count, LANES), I32),
        ],
        [
            pltpu.VMEM((2 * bag_owner.shape[1] + 16, samples), I32),
            square,
            pltpu.SemaphoreType.DMA((4,)),
        ],
        me,
        off(bag_owner.T),
        off(bag_row.T),
        off(bag_len),
        off(route.T),
        in_specs=[pl.BlockSpec(memory_space=pltpu.SMEM)] + hbm(4),
    )
    low = call(
        "cut",
        cut_kernel,
        shape((w_in.shape[1] // 2, w_in.shape[2]), BF16),
        [pltpu.SemaphoreType.DMA(())],
        off(w_in[0]),
        in_specs=hbm(1),
    )
    ins = gather_weight(w_in[0], low, plan)
    outs = gather_weight(w_out[0], w_out[0, : w_out.shape[1] // 2], plan)
    gate_t = jnp.swapaxes(gate_w, 1, 2)
    wanted = lax.all_to_all(want, both, 0, 0, tiled=True)
    row_shape = slots.shapes()[0]
    exp_shapes = eslots.shapes()
    n = len(exp_shapes)
    hot = pltpu.VMEM((slots.rows, entries), BF16)
    rows = pltpu.VMEM((slots.rows, emb), BF16)
    erows = pltpu.VMEM((eslots.rows, width), BF16)
    served = call(
        "gather",
        bind(gather_kernel, slots),
        pltpu.HBM(row_shape.shape, BF16),
        [
            pltpu.VMEM((entries, emb), F32),
            hot,
            rows,
            pltpu.VMEM(row_shape.shape, BF16),
            pltpu.SemaphoreType.DMA((1 + 4 * slots.blocks,)),
        ],
        wanted,
        off(tables.reshape(entries, emb)),
        in_specs=vmem(1) + hbm(1),
        out_specs=hbm(1)[0],
    )
    tall = call(
        "prepare",
        bind(prepare_kernel, slots, table_count),
        shape((slots.blocks, slots.rows, table_count * samples), BF16),
        [],
        plan,
    )
    returned = lax.all_to_all(served, both, 0, 0, tiled=True)
    *outgoing, first = call(
        "pool",
        bind(pool_kernel, slots, eslots, table_count),
        exp_shapes + [shape((samples, tasks), F32)],
        [rows, pltpu.VMEM((samples, width), BF16), erows],
        returned,
        plan,
        gate_t,
    )
    arrived = trade(eslots, outgoing)
    share = w_in.shape[2]
    own = [
        pltpu.VMEM((width, share), BF16),
        pltpu.VMEM((share, width), BF16),
        pltpu.SemaphoreType.DMA((2,)),
    ]
    halves = [eslots]
    if apart:
        count = expert_count // 2
        halves = [Slots(count, cap_expert, width, count, True)] * 2
    total, last, *hidden = call(
        "forward",
        bind(forward_kernel, eslots),
        [shape((eslots.rows, width), F32), shape((eslots.rows, share), BF16)]
        + [shape((4, part.rows, share), BF16) for part in halves],
        [erows] + own,
        *arrived,
        off(ins[0]),
        *ins[1:],
        off(outs[0]),
        *outs[1:5],
        in_specs=vmem(n) + hbm(1) + vmem(6) + hbm(1) + vmem(4),
    )
    result = call(
        "finish", bind(finish_kernel, eslots), exp_shapes, [erows], total, last, *outs[5:7]
    )
    back = trade(eslots, result)
    logits, dgate, *grads_out = call(
        "middle",
        bind(middle_kernel, eslots, table_count, device_count),
        [shape((tasks, samples), F32), shape((samples, width), F32)] + exp_shapes,
        [erows, pltpu.VMEM((LANES, samples), F32)],
        *back,
        plan,
        first,
        labels.T,
        head,
        gate_t,
    )
    arrived_grads = trade(eslots, grads_out)

    def back_pass(name, part, grads, kept):
        return call(
            name,
            bind(backward_kernel, part),
            part.shapes(),
            [pltpu.VMEM((part.rows, width), BF16)],
            *grads,
            kept,
            *ins,
            *outs,
        )

    if apart:
        held = call(
            "hold",
            hold_kernel,
            [pltpu.VMEM(w.shape, BF16) for w in ins + outs],
            [pltpu.SemaphoreType.DMA((14,))],
            *[off(w) for w in ins + outs],
            in_specs=hbm(14),
        )
        ins, outs = held[:7], held[7:]
        far = back_pass("backfar", halves[1], arrived_grads[count:], hidden[1])
        far = [trade_one(eslots, x, count + i) for i, x in enumerate(far)]
        near = back_pass("backnear", halves[0], arrived_grads[:count], hidden[0])
        back_grads = trade_near(eslots, near) + far
    else:
        back_grads = trade(eslots, back_pass("backward", eslots, arrived_grads, hidden[0]))
    row_out = call(
        "spread",
        bind(spread_grads_kernel, slots, eslots, table_count),
        row_shape,
        [erows, rows],
        *back_grads,
        plan,
        dgate,
        tall,
    )
    row_in = lax.all_to_all(row_out, both, 0, 0, tiled=True)
    new_tables, new_accum = call(
        "update",
        bind(update_kernel, slots),
        [shape(tables.shape, F32), shape(accum.shape, F32)],
        [pltpu.VMEM(tables.shape, F32), hot, rows, pltpu.SemaphoreType.DMA(())],
        row_in,
        wanted,
        off(tables),
        accum,
        in_specs=vmem(2) + hbm(1) + vmem(1),
    )
    return (logits.T, new_tables, new_accum)


def solution(mesh):
    in_specs = (
        P(None, ("dp", "expert"), None),
        P(None, ("dp", "expert")),
        P(("dp", "expert"), None),
        P(("dp", "expert"), None),
        P(None, ("dp", "expert")),
        P(("dp", "expert"), None),
        P(("dp", "expert"), None),
        P("expert", None, "dp"),
        P("expert", "dp", None),
        P(),
        P(),
    )
    out_specs = (
        P(("dp", "expert"), None),
        P(None, ("dp", "expert"), None),
        P(None, ("dp", "expert")),
    )

    return jax.shard_map(per_device, mesh=mesh, in_specs=in_specs, out_specs=out_specs, check_vma=False)
```

```python
import jax
import jax.numpy as jnp
from jax import lax
from jax.experimental import pallas as pl
from jax.experimental.pallas import tpu as pltpu
from jax.sharding import PartitionSpec as P


learn_rate = 0.3
norm_eps = 1e-05
LANES = 128
F32 = jnp.float32
BF16 = jnp.bfloat16
I32 = jnp.int32


GRANTS = {"gather": 16, "update": 16, "pool": 12, "prepare": 12}


def vmem(count):
    return [pl.BlockSpec(memory_space=pltpu.VMEM)] * count


def hbm(count):
    return [pl.BlockSpec(memory_space=pltpu.HBM)] * count


def params(mib):
    return pltpu.CompilerParams(vmem_limit_bytes=mib << 20)


def seq(count, body):
    if count <= 32:
        for i in range(count):
            body(i)
    else:
        lax.fori_loop(0, count, lambda i, c: (body(i), c)[1], 0)


def part(refs, o, a, b):
    return refs[o].at[a:b, :] if isinstance(refs, (list, tuple)) else refs.at[o, a:b, :]


class Slots:
    def __init__(self, peers, cap, width, group, apart=False):
        self.apart = apart
        self.peers, self.width = peers, width
        self.main, self.ext = (cap - 1, 1) if cap % 16 == 1 else (-(-cap // 16) * 16, 0)
        self.lane_blocks = width // LANES
        self.group = min(peers, group)
        self.blocks = peers // self.group
        self.rows = self.group * (self.main + self.ext)
        self.ext_units = -(-self.lane_blocks // 8) * 8 * self.ext
        self.units = self.main * self.lane_blocks + self.ext_units

    @property
    def arrays(self):
        return self.peers if self.apart else 1

    def refs(self, refs):
        return refs[0 : self.peers] if self.apart else refs[0]

    def shapes(self):
        if self.apart:
            return [jax.ShapeDtypeStruct((self.units, LANES), BF16)] * self.peers
        return [jax.ShapeDtypeStruct((self.peers, self.units, LANES), BF16)]

    def pick(self, axis):
        shape = (self.group, self.rows) if axis == 1 else (self.rows, self.group)
        c = lax.broadcasted_iota(I32, shape, axis)
        o = lax.broadcasted_iota(I32, shape, 1 - axis)
        base = o * self.main
        bulk = self.group * self.main
        own = (c >= base) & (c < base + self.main)
        rank = c - base + 1
        if self.ext:
            own = own | (c == bulk + o)
            rank = jnp.where(c < bulk, rank, self.main + 1)
        expand = jnp.where(own, 1.0, 0.0).astype(BF16)
        rank = jnp.sum(jnp.where(own, rank.astype(F32), 0.0), axis=1 - axis, keepdims=True)
        return expand, rank

    def spread(self, ranks, picks):
        expand, rank = picks
        held = jnp.dot(ranks.astype(BF16), expand, preferred_element_type=F32)
        return jnp.where(held == rank, 1.0, 0.0).astype(BF16)

    def spread_t(self, ranks, picks):
        expand, rank = picks
        held = lax.dot_general(
            expand, ranks.astype(BF16), (((1,), (1,)), ((), ())), preferred_element_type=F32
        )
        return jnp.where(held == rank, 1.0, 0.0).astype(BF16)

    def ext_pick(self, j):
        shape = (self.group * self.ext_units, self.group)
        u = lax.broadcasted_iota(I32, shape, 0)
        o = lax.broadcasted_iota(I32, shape, 1)
        return jnp.where(u == o * self.ext_units + j, 1.0, 0.0).astype(BF16)

    def pack(self, block, rows_ref, out_ref):
        self.pack_main(block, rows_ref, out_ref, range(self.group))
        self.pack_ext(block, rows_ref, out_ref)

    def pack_main(self, block, rows_ref, out_ref, peers):
        main, first = self.main, block * self.group

        def one(o):
            start = o * main if isinstance(o, int) else pl.multiple_of(o * main, 16)
            for j in range(self.lane_blocks):
                part(out_ref, first + o, j * main, (j + 1) * main)[...] = rows_ref[
                    pl.ds(start, main), j * LANES : (j + 1) * LANES
                ]

        seq(len(peers), lambda i: one(peers[0] + i))

    def pack_ext(self, block, rows_ref, out_ref):
        main, first = self.main, block * self.group
        if self.ext:
            extra = jnp.zeros((self.group * self.ext_units, LANES), F32)
            tail = rows_ref[self.group * main : self.rows, :]
            for j in range(self.lane_blocks):
                extra = extra + jnp.dot(
                    self.ext_pick(j), tail[:, j * LANES : (j + 1) * LANES], preferred_element_type=F32
                )
            for o in range(self.group):
                part(out_ref, first + o, self.lane_blocks * main, self.units)[...] = extra[
                    o * self.ext_units : (o + 1) * self.ext_units
                ].astype(BF16)

    def unpack(self, block, in_ref, rows_ref):
        main, first = self.main, block * self.group

        def one(o):
            start = o * main if isinstance(o, int) else pl.multiple_of(o * main, 16)
            for j in range(self.lane_blocks):
                rows_ref[pl.ds(start, main), j * LANES : (j + 1) * LANES] = part(
                    in_ref, first + o, j * main, (j + 1) * main
                )[...]

        seq(self.group, one)
        if self.ext:
            extra = [
                part(in_ref, first + o, self.lane_blocks * main, self.units)[...].astype(F32)
                for o in range(self.group)
            ]
            extra = jnp.concatenate(extra, axis=0).astype(BF16)
            for j in range(self.lane_blocks):
                rows_ref[self.group * main : self.rows, j * LANES : (j + 1) * LANES] = (
                    lax.dot_general(
                        self.ext_pick(j),
                        extra,
                        (((0,), (0,)), ((), ())),
                        preferred_element_type=F32,
                    ).astype(BF16)
                )


def prepare_kernel(slots, tables, plan_ref, tall_ref):
    ranks, _, _ = plan_views(plan_ref, tables, slots.peers)
    samples = plan_ref.shape[0]
    group = slots.group
    picks = slots.pick(0)
    for block in range(slots.blocks):
        for t in range(tables):
            held = ranks[t][:, block * group : (block + 1) * group]
            tall_ref[block, :, t * samples : (t + 1) * samples] = slots.spread_t(held, picks)


def one_hot_rows(slots, block, want_ref, hot_ref):
    group, main = slots.group, slots.main
    want = want_ref[block * group : (block + 1) * group, :].astype(F32)
    fill = jnp.zeros((LANES - group, LANES), F32)
    cols = jnp.concatenate([want, fill], axis=0).T
    entry = lax.broadcasted_iota(I32, (main, hot_ref.shape[1]), 1).astype(F32)
    for o in range(group):
        hit = cols[0:main, o : o + 1] == entry
        hot_ref[o * main : (o + 1) * main, :] = jnp.where(hit, 1.0, 0.0).astype(BF16)
    if slots.ext:
        entry = lax.broadcasted_iota(I32, (group, hot_ref.shape[1]), 1).astype(F32)
        hit = want[:, main : main + 1] == entry
        hot_ref[group * main : slots.rows, :] = jnp.where(hit, 1.0, 0.0).astype(BF16)


def plan_spans(columns, tables, owners):
    experts = (columns - tables * owners) // 4
    base = tables * owners
    ranks = [(t * owners, (t + 1) * owners) for t in range(tables)]
    parts = [(base + i * experts, base + (i + 1) * experts) for i in range(4)]
    return ranks, parts[0:2], parts[2:4]


def plan_views(plan_ref, tables, owners):
    plan = plan_ref[...]
    spans = plan_spans(plan.shape[1], tables, owners)
    return [[plan[:, first:last] for first, last in part] for part in spans]


def index_kernel(cap, table_rows, me_ref, owner_ref, row_ref, len_ref, route_ref, plan_ref, want_ref, stage_ref, tmp_ref, sems):
    owners = want_ref.shape[0]
    tables = len_ref.shape[0]
    columns, samples = owner_ref.shape
    ranks, eranks, ehits = plan_spans(plan_ref.shape[1], tables, owners)
    experts = eranks[0][1] - eranks[0][0]

    def keep(span, value):
        plan_ref[:, span[0] : span[1]] = value

    slots = columns // tables
    lines = (0, columns, 2 * columns, 2 * columns + 8)
    counts = (columns, columns, tables, 2)
    copies = [
        pltpu.make_async_copy(ref, stage_ref.at[line : line + count, :], sems.at[i])
        for i, (ref, line, count) in enumerate(zip((owner_ref, row_ref, len_ref, route_ref), lines, counts))
    ]
    for copy in copies:
        copy.start()
    tmp_ref[...] = jnp.zeros(tmp_ref.shape, F32)
    for copy in copies:
        copy.wait()
    for line, count in zip(lines, counts):
        tmp_ref[line : line + count, 0:samples] = stage_ref[line : line + count, :].astype(F32)
    args = tmp_ref[:, 0:samples].T
    peer = lax.broadcasted_iota(I32, (samples, owners), 1).astype(F32)
    entry = jnp.zeros((samples, owners), F32)
    named = []
    for t in range(tables):
        mine = jnp.zeros((samples, owners), F32)
        length = args[:, 2 * columns + t : 2 * columns + t + 1]
        for b in range(slots):
            j = t * slots + b
            live = jnp.where(length > float(b), args[:, j : j + 1], -1.0)
            hit = live == peer
            mine = jnp.where(hit, 1.0, mine)
            entry = jnp.where(hit, args[:, columns + j : columns + j + 1] + float(t * table_rows + 1), entry)
        named.append(mine)
    every = sum(named)
    before = (
        lax.broadcasted_iota(I32, (samples, samples), 0) > lax.broadcasted_iota(I32, (samples, samples), 1)
    )
    before = jnp.where(before, 1.0, 0.0).astype(BF16)
    rank = jnp.dot(before, every.astype(BF16), preferred_element_type=F32) + 1.0
    for t in range(tables):
        keep(ranks[t], named[t] * rank)
    rank = every * rank
    tmp_ref[...] = jnp.zeros(tmp_ref.shape, F32)
    for r in range(cap):
        tmp_ref[r : r + 1, 0:owners] = jnp.sum(
            jnp.where(rank == float(r + 1), entry, 0.0), axis=0, keepdims=True
        )
    want_ref[...] = tmp_ref[...].T[0:owners, :].astype(I32) - 1
    expert = lax.broadcasted_iota(I32, (samples, experts), 1)
    routes = [args[:, 2 * columns + 8 + k : 2 * columns + 9 + k] for k in range(2)]
    for k in range(2):
        keep(ehits[k], jnp.where(routes[k] == expert.astype(F32), 1.0, 0.0))
    expert = (expert ^ me_ref[0]).astype(F32)
    hits = [jnp.where(routes[k] == expert, 1.0, 0.0) for k in range(2)]
    rank = jnp.dot(before, (hits[0] + hits[1]).astype(BF16), preferred_element_type=F32) + 1.0
    for k in range(2):
        keep(eranks[k], hits[k] * rank)


def gather_kernel(slots, want_ref, table_ref, out_ref, held_ref, hot_ref, rows_ref, stage_ref, sems):
    load = pltpu.make_async_copy(table_ref, held_ref, sems.at[0])
    load.start()
    steps = 4 if slots.group % 4 == 0 else 1
    count = slots.group // steps
    bulk = slots.group * slots.main
    stores = []
    for block in range(slots.blocks):
        one_hot_rows(slots, block, want_ref, hot_ref)
        if block == 0:
            load.wait()
            table = held_ref[...].astype(BF16)

        def look_up(first, last):
            rows_ref[first:last, :] = jnp.dot(
                hot_ref[first:last, :], table, preferred_element_type=F32
            ).astype(BF16)

        if slots.ext:
            look_up(bulk, slots.rows)
            slots.pack_ext(block, rows_ref, stage_ref)
        for step in range(steps):
            peers = range(step * count, (step + 1) * count)
            look_up(peers[0] * slots.main, (peers[-1] + 1) * slots.main)
            slots.pack_main(block, rows_ref, stage_ref, peers)
            first = block * slots.group + peers[0]
            store = pltpu.make_async_copy(
                stage_ref.at[first : first + count],
                out_ref.at[first : first + count],
                sems.at[1 + block * steps + step],
            )
            store.start()
            stores.append(store)
    for store in stores:
        store.wait()


def pool_kernel(slots, eslots, tables, got_ref, plan_ref, gate_ref, *refs):
    out_ref = eslots.refs(refs)
    first_ref, rows_ref, feat_ref, send_ref = refs[eslots.arrays :]
    ranks, eranks, ehits = plan_views(plan_ref, tables, slots.peers)
    width = slots.width
    group = slots.group
    picks = slots.pick(1)
    sums = [0.0] * tables
    for block in range(slots.blocks):
        slots.unpack(block, got_ref, rows_ref)
        rows = rows_ref[...]
        for t in range(tables):
            held = ranks[t][:, block * group : (block + 1) * group]
            sums[t] = sums[t] + jnp.dot(slots.spread(held, picks), rows, preferred_element_type=F32)
    for t in range(tables):
        feat_ref[:, t * width : (t + 1) * width] = sums[t].astype(BF16)
    feats = feat_ref[...]
    hot = eslots.spread_t(eranks[0] + eranks[1], eslots.pick(0))
    send_ref[...] = jnp.dot(hot, feats, preferred_element_type=F32).astype(BF16)
    eslots.pack(0, send_ref, out_ref)
    for t in range(first_ref.shape[1]):
        score = lax.dot_general(feats, gate_ref[t], (((1,), (1,)), ((), ())), preferred_element_type=F32)
        z = [jnp.sum(ehits[k] * score, axis=1, keepdims=True) for k in range(2)]
        first_ref[:, t : t + 1] = jax.nn.sigmoid(z[0] - z[1])


def forward_kernel(eslots, *refs):
    n = eslots.arrays
    x_ref, refs = eslots.refs(refs), refs[n:]
    in_refs, out_refs, refs = refs[0:7], refs[7:12], refs[12:]
    total_ref, last_ref, *hidden_refs, rows_ref, in_buf, out_buf, sems = refs
    own = [
        pltpu.make_async_copy(in_refs[0], in_buf, sems.at[0]),
        pltpu.make_async_copy(out_refs[0], out_buf, sems.at[1]),
    ]
    for copy in own:
        copy.start()
    eslots.unpack(0, x_ref, rows_ref)
    rows = rows_ref[...]
    half = rows.shape[1] // 2
    share = last_ref.shape[1]
    dot = lambda a, b: jnp.dot(a, b, preferred_element_type=F32)
    total = 0.0
    for i in (1, 2, 3, 0):
        low, high = 2 * i - 1, 2 * i
        if i == 0:
            for copy in own:
                copy.wait()
            pre = dot(rows, in_buf[...])
        else:
            pre = dot(rows[:, :half], in_refs[low][...]) + dot(rows[:, half:], in_refs[high][...])
        pre = jnp.maximum(pre, 0.0)
        hidden = pre.astype(BF16)
        if i == 3:
            last_ref[...] = hidden
        count = eslots.peers // len(hidden_refs)
        bulk, extra = count * eslots.main, count * eslots.ext
        for part, ref in enumerate(hidden_refs):
            ref[i, 0:bulk, :] = hidden[part * bulk : (part + 1) * bulk]
            if extra:
                first = eslots.peers * eslots.main
                tail = pre[first : eslots.rows]
                ref[i, bulk : bulk + extra, :] = tail[part * extra : (part + 1) * extra].astype(BF16)
        if i == 0:
            total = total + dot(hidden, out_buf[...])
        elif i < 3:
            total = total + dot(hidden[:, : share // 2], out_refs[low][...])
            total = total + dot(hidden[:, share // 2 :], out_refs[high][...])
    total_ref[...] = total


def finish_kernel(eslots, total_ref, last_ref, low_ref, high_ref, *refs):
    y_ref, rows_ref = eslots.refs(refs), refs[eslots.arrays]
    hidden = last_ref[...]
    half = hidden.shape[1] // 2
    dot = lambda a, b: jnp.dot(a, b, preferred_element_type=F32)
    total = total_ref[...] + dot(hidden[:, :half], low_ref[...]) + dot(hidden[:, half:], high_ref[...])
    rows_ref[...] = total.astype(BF16)
    eslots.pack(0, rows_ref, y_ref)


def backward_kernel(eslots, *refs):
    n = eslots.arrays
    dy_ref, hidden_ref, refs = eslots.refs(refs), refs[n], refs[n + 1 :]
    in_refs, out_refs, refs = refs[0:7], refs[7:14], refs[14:]
    dx_ref = eslots.refs(refs)
    (rows_ref,) = refs[n:]
    eslots.unpack(0, dy_ref, rows_ref)
    rows = rows_ref[...]
    nt = (((1,), (1,)), ((), ()))
    half = rows.shape[1] // 2
    dot = lambda a, b: lax.dot_general(a, b, nt, preferred_element_type=F32)
    low = high = 0.0
    for i in range(4):
        parts = (0,) if i == 0 else (2 * i - 1, 2 * i)
        dhidden = [dot(rows, out_refs[p][...]) for p in parts]
        dhidden = dhidden[0] if i == 0 else jnp.concatenate(dhidden, axis=1)
        dpre = jnp.where(hidden_ref[i].astype(F32) > 0.0, dhidden, 0.0).astype(BF16)
        if i == 0:
            low, high = low + dot(dpre, in_refs[0][:half, :]), high + dot(dpre, in_refs[0][half:, :])
        else:
            low, high = low + dot(dpre, in_refs[parts[0]][...]), high + dot(dpre, in_refs[parts[1]][...])
    rows_ref[:, :half] = low.astype(BF16)
    rows_ref[:, half:] = high.astype(BF16)
    eslots.pack(0, rows_ref, dx_ref)


def hold_kernel(*refs):
    count = len(refs) // 2
    copies = [
        pltpu.make_async_copy(refs[i], refs[count + i], refs[2 * count].at[i]) for i in range(count)
    ]
    for copy in copies:
        copy.start()
    for copy in copies:
        copy.wait()


def middle_kernel(eslots, tables, owners, *refs):
    n = eslots.arrays
    y_ref, refs = eslots.refs(refs), refs[n:]
    plan_ref, first_ref, label_ref, head_ref, gate_ref, logit_ref, dgate_ref = refs[0:7]
    out_ref = eslots.refs(refs[7:])
    rows_ref, tmp_ref = refs[7 + n :]
    samples, tasks = first_ref.shape
    tmp_ref[...] = jnp.zeros(tmp_ref.shape, F32)
    tmp_ref[0:tasks, 0:samples] = label_ref[...]
    labels = tmp_ref[:, 0:samples].T
    width = eslots.width
    eslots.unpack(0, y_ref, rows_ref)
    rows = rows_ref[...]
    _, eranks, ehits = plan_views(plan_ref, tables, owners)
    picks = eslots.pick(1)
    y0, y1 = [
        jnp.dot(eslots.spread(eranks[k], picks), rows, preferred_element_type=F32) for k in range(2)
    ]
    gap = y0 - y1
    sign = ehits[0] - ehits[1]
    lane = lax.broadcasted_iota(I32, (samples, LANES), 1)
    logits = jnp.zeros((samples, LANES), F32)
    dy0 = dy1 = dgate = 0.0
    for t in range(tasks):
        g = first_ref[:, t : t + 1]
        rest = 1.0 - g
        comb = g * y0 + rest * y1
        scale = jnp.sqrt(jnp.sum(comb * comb, axis=1, keepdims=True) * (1.0 / width) + norm_eps)
        inv = 1.0 / scale
        normed = comb * inv
        head = head_ref[t : t + 1, :]
        logit = jnp.sum(normed * head, axis=1, keepdims=True)
        logits = jnp.where(lane == t, logit, logits)
        dlogit = jax.nn.sigmoid(logit) - labels[:, t : t + 1]
        drop = dlogit * logit * (1.0 / width)
        dcomb = (dlogit * head - normed * drop) * inv
        dy0 = dy0 + g * dcomb
        dy1 = dy1 + rest * dcomb
        ddelta = jnp.sum(dcomb * gap, axis=1, keepdims=True) * g * rest
        dgate = dgate + jnp.dot(
            ddelta * sign,
            gate_ref[t].astype(F32),
            precision=lax.Precision.HIGHEST,
            preferred_element_type=F32,
        )
    dgate_ref[...] = dgate
    logit_ref[...] = logits.T[0:tasks, :]
    picks = eslots.pick(0)
    send = sum(
        jnp.dot(eslots.spread_t(eranks[k], picks), dy.astype(BF16), preferred_element_type=F32)
        for k, dy in enumerate((dy0, dy1))
    )
    rows_ref[...] = send.astype(BF16)
    eslots.pack(0, rows_ref, out_ref)


def spread_grads_kernel(slots, eslots, tables, *refs):
    dx_ref, refs = eslots.refs(refs), refs[eslots.arrays :]
    plan_ref, dgate_ref, tall_ref, out_ref, rows_ref, grad_ref = refs
    _, eranks, _ = plan_views(plan_ref, tables, slots.peers)
    width = slots.width
    eslots.unpack(0, dx_ref, rows_ref)
    total = dgate_ref[...] + spread_pair(eslots, eranks, rows_ref)
    total = total.astype(BF16)
    stacked = jnp.concatenate([total[:, t * width : (t + 1) * width] for t in range(tables)], axis=0)
    for block in range(slots.blocks):
        grad_ref[...] = jnp.dot(tall_ref[block], stacked, preferred_element_type=F32).astype(BF16)
        slots.pack(block, grad_ref, out_ref)


def spread_pair(eslots, eranks, rows_ref):
    picks = eslots.pick(1)
    rows = rows_ref[...]
    hot = eslots.spread(eranks[0], picks) + eslots.spread(eranks[1], picks)
    return jnp.dot(hot, rows, preferred_element_type=F32)


def update_kernel(slots, got_ref, want_ref, table_ref, accum_ref, new_table_ref, new_accum_ref, held_ref, hot_ref, rows_ref, sem):
    copy = pltpu.make_async_copy(table_ref, held_ref, sem)
    copy.start()
    tables, table_rows = accum_ref.shape
    width = slots.width
    grads = 0.0
    for block in range(slots.blocks):
        one_hot_rows(slots, block, want_ref, hot_ref)
        slots.unpack(block, got_ref, rows_ref)
        grads = grads + lax.dot_general(
            rows_ref[...], hot_ref[...], (((0,), (0,)), ((), ())), preferred_element_type=F32
        )
    copy.wait()
    for t in range(tables):
        part = grads[:, t * table_rows : (t + 1) * table_rows]
        total = accum_ref[t : t + 1, :] + jnp.sum(part * part, axis=0, keepdims=True) * (1.0 / width)
        new_accum_ref[t : t + 1, :] = total
        step = part * (learn_rate / jnp.sqrt(total))
        new_table_ref[t] = held_ref[t] - step.T


def cut_kernel(w_ref, out_ref, sem):
    copy = pltpu.make_async_copy(w_ref.at[0 : out_ref.shape[0]], out_ref, sem)
    copy.start()
    copy.wait()


def gather_weight(w, low, later):
    half = w.shape[0] // 2

    def send(x, bit):
        return lax.ppermute(x, "dp", [(i, i ^ bit) for i in range(4)])

    high = lax.optimization_barrier((w, later))[0][half:]
    low1, low2 = send(low, 1), send(low, 2)
    high1, high2 = send(high, 1), send(high, 2)
    return [w, low1, high1, low2, high2, send(low1, 2), send(high2, 1)]


def trade_one(eslots, chunk, k):
    return lax.ppermute(chunk, "expert", [(i, i ^ k) for i in range(eslots.peers)])


def trade(eslots, chunks):
    if not eslots.apart:
        return [lax.all_to_all(chunks[0], "expert", 0, 0, tiled=True)]
    got = {0: chunks[0]}
    for k in sorted(range(1, eslots.peers), key=lambda k: (-(k // 2), k)):
        got[k] = trade_one(eslots, chunks[k], k)
    return [got[k] for k in range(eslots.peers)]


def trade_near(eslots, chunks):
    return [chunks[0]] + [trade_one(eslots, x, k + 1) for k, x in enumerate(chunks[1:])]


def per_device(
    tables, accum, bag_owner, bag_row, bag_len, route, labels, w_in, w_out, gate_w, head
):
    dp_count = lax.axis_size("dp")
    expert_count = lax.axis_size("expert")
    device_count = dp_count * expert_count
    samples = route.shape[0]
    table_count, table_rows, emb = tables.shape
    entries = table_count * table_rows
    lookups = samples * bag_owner.shape[1]
    width = table_count * emb
    tasks = labels.shape[1]
    cap_rows = (5 * lookups + 4 * device_count - 1) // (4 * device_count) + 1
    cap_expert = (2 * samples + expert_count - 1) // expert_count + 1
    slots = Slots(device_count, cap_rows, emb, 32)
    apart = expert_count <= 8
    eslots = Slots(expert_count, cap_expert, width, expert_count, apart)
    shape = jax.ShapeDtypeStruct
    both = ("dp", "expert")
    me = lax.axis_index("expert").astype(I32) if apart else jnp.int32(0)
    me = me.reshape(1)

    def off(x):
        return pltpu.with_memory_space_constraint(x, pltpu.HBM)

    def call(name, kernel, out_shape, scratch, *args, in_specs=None, out_specs=None):
        many = isinstance(out_shape, (list, tuple))
        return pl.pallas_call(
            kernel,
            out_shape=out_shape,
            in_specs=in_specs or vmem(len(args)),
            out_specs=out_specs or (vmem(len(out_shape)) if many else vmem(1)[0]),
            scratch_shapes=scratch,
            compiler_params=params(GRANTS.get(name, 8) if eslots.rows <= 512 else 60),
        )(*args)

    def bind(fn, *static):
        return lambda *refs: fn(*static, *refs)

    square = pltpu.VMEM((LANES, max(LANES, device_count)), F32)
    plan, want = call(
        "index",
        bind(index_kernel, cap_rows, table_rows),
        [
            shape((samples, table_count * device_count + 4 * expert_count), F32),
            shape((device_count, LANES), I32),
        ],
        [
            pltpu.VMEM((2 * bag_owner.shape[1] + 16, samples), I32),
            square,
            pltpu.SemaphoreType.DMA((4,)),
        ],
        me,
        off(bag_owner.T),
        off(bag_row.T),
        off(bag_len),
        off(route.T),
        in_specs=[pl.BlockSpec(memory_space=pltpu.SMEM)] + hbm(4),
    )
    low = call(
        "cut",
        cut_kernel,
        pltpu.VMEM((w_in.shape[1] // 2, w_in.shape[2]), BF16),
        [pltpu.SemaphoreType.DMA(())],
        off(w_in[0]),
        in_specs=hbm(1),
    )
    ins = gather_weight(w_in[0], low, plan)
    outs = gather_weight(w_out[0], w_out[0, : w_out.shape[1] // 2], plan)
    gate_t = jnp.swapaxes(gate_w, 1, 2)
    wanted = lax.all_to_all(want, both, 0, 0, tiled=True)
    row_shape = slots.shapes()[0]
    exp_shapes = eslots.shapes()
    n = len(exp_shapes)
    hot = pltpu.VMEM((slots.rows, entries), BF16)
    rows = pltpu.VMEM((slots.rows, emb), BF16)
    erows = pltpu.VMEM((eslots.rows, width), BF16)
    served = call(
        "gather",
        bind(gather_kernel, slots),
        pltpu.HBM(row_shape.shape, BF16),
        [
            pltpu.VMEM((entries, emb), F32),
            hot,
            rows,
            pltpu.VMEM(row_shape.shape, BF16),
            pltpu.SemaphoreType.DMA((1 + 4 * slots.blocks,)),
        ],
        wanted,
        off(tables.reshape(entries, emb)),
        in_specs=vmem(1) + hbm(1),
        out_specs=hbm(1)[0],
    )
    tall = call(
        "prepare",
        bind(prepare_kernel, slots, table_count),
        shape((slots.blocks, slots.rows, table_count * samples), BF16),
        [],
        plan,
    )
    returned = lax.all_to_all(served, both, 0, 0, tiled=True)
    *outgoing, first = call(
        "pool",
        bind(pool_kernel, slots, eslots, table_count),
        exp_shapes + [shape((samples, tasks), F32)],
        [rows, pltpu.VMEM((samples, width), BF16), erows],
        returned,
        plan,
        gate_t,
    )
    arrived = trade(eslots, outgoing)
    share = w_in.shape[2]
    own = [
        pltpu.VMEM((width, share), BF16),
        pltpu.VMEM((share, width), BF16),
        pltpu.SemaphoreType.DMA((2,)),
    ]
    halves = [eslots]
    if apart:
        count = expert_count // 2
        halves = [Slots(count, cap_expert, width, count, True)] * 2

    def hold(name, arrays):
        return call(
            name,
            hold_kernel,
            [pltpu.VMEM(w.shape, BF16) for w in arrays],
            [pltpu.SemaphoreType.DMA((len(arrays),))],
            *[off(w) for w in arrays],
            in_specs=hbm(len(arrays)),
        )

    if apart:
        ins[1:] = hold("holdin", ins[1:])
    total, last, *hidden = call(
        "forward",
        bind(forward_kernel, eslots),
        [shape((eslots.rows, width), F32), shape((eslots.rows, share), BF16)]
        + [shape((4, part.rows, share), BF16) for part in halves],
        [erows] + own,
        *arrived,
        off(ins[0]),
        *ins[1:],
        off(outs[0]),
        *outs[1:5],
        in_specs=vmem(n) + hbm(1) + vmem(6) + hbm(1) + vmem(4),
    )
    result = call(
        "finish", bind(finish_kernel, eslots), exp_shapes, [erows], total, last, *outs[5:7]
    )
    back = trade(eslots, result)
    logits, dgate, *grads_out = call(
        "middle",
        bind(middle_kernel, eslots, table_count, device_count),
        [shape((tasks, samples), F32), shape((samples, width), F32)] + exp_shapes,
        [erows, pltpu.VMEM((LANES, samples), F32)],
        *back,
        plan,
        first,
        labels.T,
        head,
        gate_t,
    )
    arrived_grads = trade(eslots, grads_out)

    def back_pass(name, part, grads, kept):
        return call(
            name,
            bind(backward_kernel, part),
            part.shapes(),
            [pltpu.VMEM((part.rows, width), BF16)],
            *grads,
            kept,
            *ins,
            *outs,
        )

    if apart:
        held = hold("hold", [ins[0]] + outs)
        ins, outs = [held[0]] + list(ins[1:]), held[1:]
        far = back_pass("backfar", halves[1], arrived_grads[count:], hidden[1])
        far = [trade_one(eslots, x, count + i) for i, x in enumerate(far)]
        near = back_pass("backnear", halves[0], arrived_grads[:count], hidden[0])
        back_grads = trade_near(eslots, near) + far
    else:
        back_grads = trade(eslots, back_pass("backward", eslots, arrived_grads, hidden[0]))
    row_out = call(
        "spread",
        bind(spread_grads_kernel, slots, eslots, table_count),
        row_shape,
        [erows, rows],
        *back_grads,
        plan,
        dgate,
        tall,
    )
    row_in = lax.all_to_all(row_out, both, 0, 0, tiled=True)
    new_tables, new_accum = call(
        "update",
        bind(update_kernel, slots),
        [shape(tables.shape, F32), shape(accum.shape, F32)],
        [pltpu.VMEM(tables.shape, F32), hot, rows, pltpu.SemaphoreType.DMA(())],
        row_in,
        wanted,
        off(tables),
        accum,
        in_specs=vmem(2) + hbm(1) + vmem(1),
    )
    return (logits.T, new_tables, new_accum)


def solution(mesh):
    in_specs = (
        P(None, ("dp", "expert"), None),
        P(None, ("dp", "expert")),
        P(("dp", "expert"), None),
        P(("dp", "expert"), None),
        P(None, ("dp", "expert")),
        P(("dp", "expert"), None),
        P(("dp", "expert"), None),
        P("expert", None, "dp"),
        P("expert", "dp", None),
        P(),
        P(),
    )
    out_specs = (
        P(("dp", "expert"), None),
        P(None, ("dp", "expert"), None),
        P(None, ("dp", "expert")),
    )

    return jax.shard_map(per_device, mesh=mesh, in_specs=in_specs, out_specs=out_specs, check_vma=False)
```
